256 devices in a mesh: slab: 64 (over x_lo, z, y), coil: 4 (over x_hi, core).
Axes of the slice: x: 4 (x_hi: 2, x_lo: 2; x = x_hi * 2 + x_lo), y: 4, z: 8, core: 2. Of those that a mesh axis runs over, the one named last changes fastest.
Arguments:
- init_image: float32 [2, 64, 256, 256], P(None, 'coil', 'slab'), may hold values from -6 to 6
- sens: float32 [2, 8, 64, 256, 256], P(None, 'coil', None, 'slab'), may hold values from -1.5 to 1.5
- kspace: float32 [2, 8, 64, 256, 256], P(None, 'coil', 'slab'), may hold values from -6 to 6
- mask: int32 [256, 256], replicated, may hold values 0 or 1
- weights: float32 [1, 48, 2, 3, 3, 3], replicated, may hold values from -0.3125 to 0.3125
- step_sizes: float32 [1], replicated, may hold values from 0.5 to 2
- recon_cotangent: float32 [2, 64, 256, 256], P(None, 'coil', 'slab'), may hold values from -0.009 to 0.009
Outputs:
- recon: float32 [2, 64, 256, 256], P(None, 'coil', 'slab')
- filter_grads: float32 [1, 48, 2, 3, 3, 3], replicated
- step_grads: float32 [1], replicated
The draws below stay inside these ranges and needn't reach their ends.
All inputs are finite; a program needn't handle non-finite values.
Results may differ from the reference program's by a relative error of at most 0.0003.
Values sent between devices are 32-bit elements; how exact they have to be, the bound alone decides.
No kernel may reach another device: no remote copies, remote signals or barrier semaphores. Data moves between devices by JAX's collectives and lax.ppermute only.
A program may use at most 128 MiB of HBM per device.

```python
import math
import jax
import jax.numpy as jnp
from jax import lax

KY = 256
KZ = 256
COILS = 8
FEAT = 48
CASC = 1
R = 64


def touch_ends(result, stream_key, least, top_value):
    longest = result.shape.index(max(result.shape))
    spots = []
    for shift in (0, 1):
        where = [jax.random.randint(jax.random.fold_in(stream_key, axis), (), 0, length) for axis, length in enumerate(result.shape)]
        where[longest] = (where[longest] + shift) % result.shape[longest]
        spots.append(tuple(where))
    return result.at[spots[0]].set(least).at[spots[1]].set(top_value)


def levels(stream_key, dims, cuts, smallest, top_value):
    gain, own = 1.0, jax.random.fold_in(stream_key, 6)
    for dim, parts in cuts:
        heights = jnp.exp(jax.random.uniform(jax.random.fold_in(own, dim), (parts,), jnp.float32, smallest / len(cuts), top_value / len(cuts)))
        gain = gain * jnp.repeat(heights, dims[dim] // parts).reshape([-1 if axis == dim else 1 for axis in range(len(dims))])
    return gain


def scatter_about(stream_key, extent, width, most, cuts=(), kind=jnp.bfloat16):
    gain = levels(stream_key, extent, cuts, -0.22, 0.18) if cuts else 1.0
    array = jax.random.normal(stream_key, extent, jnp.float32) * width * gain
    return jnp.minimum(jnp.maximum(array, -most), most).astype(kind)


def setup_inputs(seed: int = 0) -> dict:
    keys = jax.random.split(jax.random.key(seed), 8)
    init_image = scatter_about(keys[0], (2, R, KY, KZ), 1.0, 6.0, ((1, 4), (2, 64)), jnp.float32)
    sens = scatter_about(keys[1], (2, COILS, R, KY, KZ), 0.25, 1.5, ((1, 4), (3, 64)), jnp.float32)
    kspace = scatter_about(keys[2], (2, COILS, R, KY, KZ), 1.0, 6.0, ((1, 4), (2, 64)), jnp.float32)
    mask = touch_ends((jax.random.randint(keys[3], (KY, KZ), 0, 3) < 1).astype(jnp.int32), jax.random.fold_in(keys[3], 1), 0, 1)
    weights = scatter_about(keys[4], (CASC, FEAT, 2, 3, 3, 3), 432 ** -0.5, 0.3125, (), jnp.float32)
    step_sizes = jnp.clip(jnp.exp(jax.random.uniform(keys[5], (CASC,), jnp.float32, math.log(0.5), math.log(2.0))), 0.5, 2.0)
    recon_cotangent = scatter_about(keys[6], (2, R, KY, KZ), 0.0015, 0.009, ((1, 4), (2, 64)), jnp.float32)
    return {"init_image": init_image, "sens": sens, "kspace": kspace, "mask": mask, "weights": weights, "step_sizes": step_sizes, "recon_cotangent": recon_cotangent}


def normal_op(image, sens, kspace, mask, subtract):
    maps = lax.complex(sens[0], sens[1])
    coils = maps * lax.complex(image[0], image[1])[None]
    spectrum = jnp.fft.fftn(coils, axes=(2, 3), norm="ortho")
    if subtract:
        spectrum = spectrum - lax.complex(kspace[0], kspace[1])
    spectrum = spectrum * mask.astype(jnp.float32)
    back = jnp.fft.ifftn(spectrum, axes=(2, 3), norm="ortho")
    total = jnp.sum(jnp.conj(maps) * back, axis=0)
    return jnp.stack([jnp.real(total), jnp.imag(total)])


def conv_forward(field, filters):
    return lax.conv_general_dilated(field[None], filters, (1, 1, 1), ((1, 1), (1, 1), (1, 1)),
                                    dimension_numbers=("NCDHW", "OIDHW", "NCDHW"),
                                    precision=lax.Precision.HIGHEST)[0]


def conv_adjoint(field, filters):
    turned = jnp.flip(filters, (2, 3, 4)).transpose(1, 0, 2, 3, 4)
    return conv_forward(field, turned)


def correlate(left, right):
    padded = jnp.pad(right, ((0, 0), (1, 1), (1, 1), (1, 1)))
    size_r, size_y, size_z = left.shape[1], left.shape[2], left.shape[3]
    terms = []
    for shift_r in range(3):
        for shift_y in range(3):
            for shift_z in range(3):
                window = padded[:, shift_r:shift_r + size_r, shift_y:shift_y + size_y, shift_z:shift_z + size_z]
                terms.append(jnp.einsum("orsz,irsz->oi", left, window, precision=lax.Precision.HIGHEST))
    stacked = jnp.stack(terms, axis=-1)
    return stacked.reshape(left.shape[0], right.shape[0], 3, 3, 3)


def regularize(state, filters):
    blocks = filters.reshape(-1, 8, 2, 3, 3, 3)

    def single(block):
        return conv_adjoint(jnp.tanh(conv_forward(state, block)), block)

    return jnp.sum(lax.map(single, blocks), axis=0)


def regularize_back(state, grad, filters):
    blocks = filters.reshape(-1, 8, 2, 3, 3, 3)

    def single(block):
        active = jnp.tanh(conv_forward(state, block))
        weighted = (1.0 - active * active) * conv_forward(grad, block)
        back = conv_adjoint(weighted, block)
        return back, correlate(active, grad) + correlate(weighted, state)

    backs, grads = lax.map(single, blocks)
    return jnp.sum(backs, axis=0), grads.reshape(filters.shape)


def reference(init_image, sens, kspace, mask, weights, step_sizes, recon_cotangent):
    state = init_image
    saved = []
    for cascade in range(CASC):
        combined = normal_op(state, sens, kspace, mask, True)
        saved.append((state, combined))
        state = state - regularize(state, weights[cascade]) - step_sizes[cascade] * combined
    recon = state
    grad = recon_cotangent
    filter_list = [None] * CASC
    step_list = [None] * CASC
    for cascade in reversed(range(CASC)):
        prior, combined = saved[cascade]
        step_list[cascade] = -jnp.sum(grad * combined)
        normal = normal_op(grad, sens, kspace, mask, False)
        back, filter_grad = regularize_back(prior, grad, weights[cascade])
        filter_list[cascade] = -filter_grad
        grad = grad - back - step_sizes[cascade] * normal
    return recon, jnp.stack(filter_list), jnp.stack(step_list)
```

```python
import jax
import jax.numpy as jnp
import numpy as np
from jax import lax
from jax.sharding import PartitionSpec as P

HIGH = lax.Precision.HIGH
AXES = ("slab", "coil")


def fourier_tables(length):
    index = np.arange(length)
    angles = (index[:, None] * index[None, :] % length) * (2.0 * np.pi / length)
    factor = 1.0 / np.sqrt(length)
    return (
        np.asarray(np.cos(angles) * factor, np.float32),
        np.asarray(np.sin(angles) * factor, np.float32),
    )


def rows_times(table, data):
    return jnp.einsum("kn,...nz->...kz", table, data, precision=HIGH)


def times_depth(data, table):
    return jnp.einsum("...n,nk->...k", data, table, precision=HIGH)


def device(coil, quarter, low):
    return (quarter * 16 + low) * 4 + coil


def spread_pairs(turn):
    return [
        (device(c, q, low), device((q + turn) % 4, c, low))
        for c in range(4)
        for q in range(4)
        for low in range(16)
    ]


def return_pairs(turn):
    return [
        (device(c, b, low), device(b, (c + turn) % 4, low))
        for c in range(4)
        for b in range(4)
        for low in range(16)
    ]


def rotated(pieces, start):
    twice = jnp.concatenate([pieces, pieces], axis=0)
    return lax.dynamic_slice_in_dim(twice, start, 4, axis=0)


def data_term(received, kspace, sampled, coil):
    cosine, sine = fourier_tables(256)
    own = received[:, 4].reshape(64, 2, 2, 256)
    state_rows = own[:, 0]
    pieces = jnp.stack(
        [lax.ppermute(state_rows, AXES, spread_pairs(turn)) for turn in range(4)]
    )
    reverse = jnp.stack([pieces[0], pieces[3], pieces[2], pieces[1]])
    image = rotated(reverse, (4 - coil) % 4)
    image = image.transpose(2, 1, 0, 3).reshape(2, 1, 256, 256)
    maps = received[:, :4].reshape(256, 2, 2, 256).transpose(1, 2, 0, 3)
    re = maps[0] * image[0] - maps[1] * image[1]
    im = maps[0] * image[1] + maps[1] * image[0]
    ur = times_depth(re, cosine) + times_depth(im, sine)
    ui = times_depth(im, cosine) - times_depth(re, sine)
    vr = rows_times(cosine, ur) + rows_times(sine, ui)
    vi = rows_times(cosine, ui) - rows_times(sine, ur)
    vr = (vr - kspace[0, :, 0]) * sampled
    vi = (vi - kspace[1, :, 0]) * sampled
    wr = rows_times(cosine, vr) - rows_times(sine, vi)
    wi = rows_times(cosine, vi) + rows_times(sine, vr)
    xr = times_depth(wr, cosine) - times_depth(wi, sine)
    xi = times_depth(wi, cosine) + times_depth(wr, sine)
    back_re = jnp.sum(maps[0] * xr + maps[1] * xi, axis=0)
    back_im = jnp.sum(maps[0] * xi - maps[1] * xr, axis=0)
    parts = jnp.stack([back_re, back_im]).reshape(2, 64, 4, 256).transpose(2, 1, 0, 3)
    total = 0.0
    for turn in range(4):
        part = lax.dynamic_index_in_dim(parts, (coil + turn) % 4, 0, keepdims=False)
        total = total + lax.ppermute(part, AXES, return_pairs(turn))
    return total, jnp.sum(total * own[:, 1])


def halos(state, grad, slab_count):
    up = [(i, i + 1) for i in range(slab_count - 1)]
    down = [(i + 1, i) for i in range(slab_count - 1)]
    high = jnp.concatenate([state[:, :, 2:], grad[:, :, 3:]], axis=2)
    low = jnp.concatenate([state[:, :, :2], grad[:, :, :1]], axis=2)
    before = lax.ppermute(high, "slab", up)
    after = lax.ppermute(low, "slab", down)
    state = jnp.concatenate([before[:, :, :2], state, after[:, :, :2]], axis=2)
    grad = jnp.concatenate([before[:, :, 2:], grad, after[:, :, 2:]], axis=2)
    up = [(i, i + 1) for i in range(3)]
    down = [(i + 1, i) for i in range(3)]
    spare = ((0, 0), (0, 2), (0, 0))
    high = jnp.concatenate(
        [state[:, 14:].reshape(4, 8, 256), jnp.pad(grad[:, 15], spare)], axis=0
    )
    low = jnp.concatenate(
        [state[:, :2].reshape(4, 8, 256), jnp.pad(grad[:, 0], spare)], axis=0
    )
    before = lax.ppermute(high, "coil", up)
    after = lax.ppermute(low, "coil", down)
    state = jnp.concatenate(
        [before[:4].reshape(2, 2, 8, 256), state, after[:4].reshape(2, 2, 8, 256)], axis=1
    )
    grad = jnp.concatenate([before[4:, None, :6], grad, after[4:, None, :6]], axis=1)
    return state, grad


def patches(padded):
    rows = padded.shape[1] - 2
    columns = padded.shape[2] - 2
    wide = jnp.pad(padded, ((0, 0), (0, 0), (0, 0), (1, 1)))
    pieces = [
        wide[:, r : r + rows, c : c + columns, d : d + 256]
        for r in range(3)
        for c in range(3)
        for d in range(3)
    ]
    return jnp.stack(pieces, axis=1).reshape(54, rows, columns, 256)


def transpose_conv(cycle, filters):
    wide = jnp.pad(cycle, ((0, 0), (0, 0), (0, 0), (1, 1)))
    product = jnp.einsum("fk,fuvz->kuvz", filters, wide, precision=HIGH)
    product = product.reshape(2, 3, 3, 3, 18, 6, 258)
    total = 0.0
    for r in range(3):
        for c in range(3):
            for d in range(3):
                total = total + product[
                    :, r, c, d, 2 - r : 18 - r, 2 - c : 6 - c, 2 - d : 258 - d
                ]
    return total


def inside(count, index, parts):
    place = index * count - 1 + jnp.arange(count + 2)
    return ((place >= 0) & (place < count * parts)).astype(jnp.float32)


def on_device(init_image, sens, kspace, mask, weights, step_sizes, recon_cotangent):
    slab_count = lax.axis_size("slab")
    coil = lax.axis_index("coil")
    slab = lax.axis_index("slab")
    sampled = mask.astype(jnp.float32)
    maps = sens.transpose(2, 3, 0, 1, 4).reshape(64, 4, 4, 256)
    images = jnp.stack([init_image, recon_cotangent]).transpose(3, 2, 0, 1, 4)
    payload = jnp.concatenate([maps, images.reshape(64, 1, 4, 256)], axis=1)
    received = lax.all_to_all(payload, "slab", split_axis=0, concat_axis=0, tiled=True)

    filters = weights[0].reshape(48, 54)
    state, grad = halos(init_image, recon_cotangent, slab_count)
    stack_state = patches(state)
    stack_grad = patches(grad)
    response = jnp.einsum("fk,kuvz->fuvz", filters, stack_state, precision=HIGH)
    keep = inside(16, coil, 4)[:, None] * inside(4, slab, 64)[None, :]
    active = jnp.tanh(response) * keep[:, :, None]
    linear = jnp.einsum("fk,kuvz->fuvz", filters, stack_grad, precision=HIGH)
    core = active[:, 1:17, 1:5]
    weighted = (1.0 - core * core) * linear
    first = jnp.einsum("fuvz,kuvz->fk", core, stack_grad, precision=HIGH)
    second = jnp.einsum(
        "fuvz,kuvz->fk", weighted, stack_state[:, 1:17, 1:5], precision=HIGH
    )
    partial = jnp.pad(-(first + second).reshape(2592), (0, 224)).reshape(256, 11)
    chunk = jnp.sum(
        lax.all_to_all(partial, AXES, split_axis=0, concat_axis=0, tiled=True), axis=0
    )
    regular = transpose_conv(active, filters)

    total, product = data_term(received, kspace, sampled, coil)
    rider = jnp.concatenate([chunk, -product[None], jnp.zeros((244,), jnp.float32)])
    sent = jnp.concatenate(
        [total, jnp.broadcast_to(rider[None, None], (64, 1, 256))], axis=1
    )
    arrived = lax.all_to_all(sent, "slab", split_axis=0, concat_axis=0, tiled=True)
    combined = arrived[:, :2].reshape(4, 16, 2, 256).transpose(2, 1, 0, 3)
    recon = init_image - regular - step_sizes[0] * combined
    riders = arrived[:, 2, :12]
    small = jnp.concatenate([riders[:, :11].reshape(704), jnp.sum(riders[:, 11])[None]])
    small = jnp.pad(small, (0, 319)).reshape(8, 128)
    others = [small] + [
        lax.ppermute(small, "coil", [(i, (i + turn) % 4) for i in range(4)])
        for turn in range(1, 4)
    ]
    reverse = jnp.stack([others[0], others[3], others[2], others[1]])
    ordered = rotated(reverse, (4 - coil) % 4).reshape(4, 1024)
    step_grads = jnp.sum(ordered[:, 704])[None]
    grads = ordered[:, :704].reshape(4, 64, 11).transpose(1, 0, 2).reshape(2816)[:2592]
    return recon, grads.reshape(weights.shape), step_grads


def solution(mesh):
    return jax.shard_map(
        on_device,
        mesh=mesh,
        in_specs=(
            P(None, "coil", "slab", None),
            P(None, "coil", None, "slab", None),
            P(None, "coil", "slab", None, None),
            P(),
            P(),
            P(),
            P(None, "coil", "slab", None),
        ),
        out_specs=(P(None, "coil", "slab", None), P(), P()),
        check_vma=False,
    )
```

```python
import jax
import jax.numpy as jnp
import numpy as np
from jax import lax
from jax.experimental import pallas as pl
from jax.experimental.pallas import tpu as pltpu
from jax.sharding import PartitionSpec as P

AXES = ("slab", "coil")
BF = jnp.bfloat16
F32 = jnp.float32


def device(coil, quarter, low):
    return (quarter * 16 + low) * 4 + coil


def spread_pairs(turn):
    return [
        (device(c, q, low), device((q + turn) % 4, c, low))
        for c in range(4)
        for q in range(4)
        for low in range(16)
    ]


def return_pairs(turn):
    return [
        (device(c, b, low), device(b, (c + turn) % 4, low))
        for c in range(4)
        for b in range(4)
        for low in range(16)
    ]


def rotated(pieces, start):
    twice = jnp.concatenate([pieces, pieces], axis=0)
    return lax.dynamic_slice_in_dim(twice, start, 4, axis=0)


def split(value):
    high = value.astype(BF)
    return high, (value - high.astype(F32)).astype(BF)


def split_outside(value):
    high = lax.reduce_precision(value, 8, 7)
    return high.astype(BF), (value - high).astype(BF)


def shifted(value, step):
    if step == 0:
        return value
    lane = lax.broadcasted_iota(jnp.int32, value.shape, value.ndim - 1)
    turned = pltpu.roll(value, step % 256, value.ndim - 1)
    edge = 0 if step > 0 else 255
    return jnp.where(lane == edge, 0.0, turned)


def filter_tables(weights):
    taps = np.zeros((3, 6, 8), np.float32)
    for d in range(3):
        for y in range(6):
            taps[d, y, y + d] = 1.0
    kernel = weights[0]
    ahead = sum(
        kernel[:, :, :, d][:, :, :, :, None, None] * taps[d] for d in range(3)
    )
    ahead = ahead.transpose(4, 0, 3, 2, 1, 5).reshape(288, 144)
    back = np.zeros((3, 4, 6), np.float32)
    for d in range(3):
        for y in range(4):
            back[d, y, y + 2 - d] = 1.0
    behind = sum(
        kernel[:, :, :, d][:, :, :, :, None, None] * back[d] for d in range(3)
    )
    behind = behind.transpose(2, 3, 1, 4, 5, 0).reshape(72, 288)
    high, low = split_outside(ahead)
    wide = jnp.concatenate([high, low, high], axis=1)
    high, low = split_outside(behind)
    turned = jnp.concatenate(
        [
            jnp.concatenate([high, high], axis=1),
            jnp.concatenate([low, jnp.zeros_like(low)], axis=1),
        ],
        axis=0,
    )
    return wide, turned


def conv_kernel(
    edge, init, grad, before, after, lower, upper, wide, turned, base, sums,
    xs, gs, xb, gb, acc,
):
    gs[:, :, 0:1] = jnp.zeros((18, 2, 1, 256), F32)
    gs[:, :, 7:8] = jnp.zeros((18, 2, 1, 256), F32)
    for i in range(2):
        xs[2:18, i, 2:6] = init[i]
        xs[2:18, i, 0:2] = before[i, :, 0:2]
        xs[2:18, i, 6:8] = after[i, :, 0:2]
        xs[0:2, i] = lower[2 * i : 2 * i + 2]
        xs[18:20, i] = upper[2 * i : 2 * i + 2]
        gs[1:17, i, 2:6] = grad[i]
        gs[1:17, i, 1:2] = before[i, :, 2:3]
        gs[1:17, i, 6:7] = after[i, :, 2:3]
        gs[0:1, i, 1:7] = lower[4 + i : 5 + i, 0:6]
        gs[17:18, i, 1:7] = upper[4 + i : 5 + i, 0:6]
    for plain, packed, count in ((xs, xb, 320), (gs, gb, 288)):
        value = plain[...].reshape(count, 256)
        for d in range(3):
            high, low = split(shifted(value, 1 - d))
            packed[d, 0] = high
            packed[d, 1] = low
    acc[...] = jnp.zeros_like(acc)
    sums[...] = jnp.zeros_like(sums)
    row = lax.broadcasted_iota(jnp.int32, (288, 256), 0)
    keep = jnp.where(row < 48, edge[0], jnp.where(row >= 240, edge[1], 1.0))

    def window(packed, place, part):
        start = pl.multiple_of(place * 16, 16)
        return jnp.concatenate(
            [packed[d, part, pl.ds(start, 48)] for d in range(3)], axis=0
        )

    def forward(place, table, packed):
        high = window(packed, place, 0)
        low = window(packed, place, 1)
        data = jnp.concatenate([high, high, low], axis=0)
        return jnp.dot(table, data, preferred_element_type=F32), high, low

    def scatter(place, high, low):
        data = jnp.concatenate([high, low], axis=0)
        product = jnp.dot(turned[...], data, preferred_element_type=F32)
        product = product[:72] + product[72:]
        for r in range(3):
            for d in range(3):
                first = (r * 3 + d) * 8
                acc[d, pl.ds(place + r, 1)] += product[first : first + 8][None]

    for place, scale in ((0, edge[2]), (17, edge[3])):
        response, _, _ = forward(place, wide[...], xb)
        high, low = split(jnp.tanh(response) * (keep * scale))
        scatter(place, high, low)

    def step(r, carry):
        response, xh, xl = forward(r + 1, wide[...], xb)
        linear, gh, gl = forward(r, wide[48:240], gb)
        active = jnp.tanh(response) * keep
        core = active[48:240]
        weighted = (1.0 - core * core) * linear
        high, low = split(active)
        wh, wl = split(weighted)
        ch, cl = high[48:240], low[48:240]
        left = jnp.concatenate([gh, gh, gl, xh, xh, xl], axis=1)
        right = jnp.concatenate([ch, cl, ch, wh, wl, wh], axis=1)
        sums[...] += lax.dot_general(
            left, right, (((1,), (1,)), ((), ())), preferred_element_type=F32
        )
        scatter(r + 1, high, low)
        return carry

    lax.fori_loop(0, 16, step, 0)
    total = (
        shifted(acc[0, 2:18].reshape(128, 256), -1)
        + acc[1, 2:18].reshape(128, 256)
        + shifted(acc[2, 2:18].reshape(128, 256), 1)
    ).reshape(16, 8, 256)
    for i in range(2):
        base[i] = init[i] - total[:, 4 * i : 4 * i + 4]


def conv_call(edge, init, grad, before, after, lower, upper, wide, turned):
    vm = pl.BlockSpec(memory_space=pltpu.VMEM)
    return pl.pallas_call(
        conv_kernel,
        out_shape=(
            jax.ShapeDtypeStruct((2, 16, 4, 256), F32),
            jax.ShapeDtypeStruct((144, 192), F32),
        ),
        in_specs=[pl.BlockSpec(memory_space=pltpu.SMEM)] + [vm] * 8,
        out_specs=(vm, vm),
        scratch_shapes=[
            pltpu.VMEM((20, 2, 8, 256), F32),
            pltpu.VMEM((18, 2, 8, 256), F32),
            pltpu.VMEM((3, 2, 320, 256), BF),
            pltpu.VMEM((3, 2, 288, 256), BF),
            pltpu.VMEM((3, 20, 8, 256), F32),
        ],
        cost_estimate=pl.CostEstimate(
            flops=6000000000, bytes_accessed=2000000, transcendentals=1300000
        ),
    )(edge, init, grad, before, after, lower, upper, wide, turned)


def diagonal(sums):
    cube = sums.reshape(3, 3, 2, 8, 4, 48)
    taps = [
        sum(cube[:, :, :, y + 1 + d, y] for y in range(4)) for d in range(3)
    ]
    return jnp.stack(taps, axis=3)


def tables():
    place = np.arange(256)
    mixed = place % 64 * 4 + place // 64
    made = []
    for first, second in ((place, place), (place, mixed), (mixed, place)):
        angle = (first[:, None] * second[None, :] % 256) * (2.0 * np.pi / 256)
        for table in (np.cos(angle) / 16.0, np.sin(angle) / 16.0):
            table = np.asarray(table, np.float32)
            high = table.astype(BF)
            made.append(high)
            made.append((table - high.astype(np.float32)).astype(BF))
    return made


def transform_kernel(
    coil, maps, p0, p1, p2, p3, kspace, mask, ch, cl, sh, sl, yh, yl, zh, zl,
    uh, ul, wh, wl, o0, o1, o2, o3, rows, right, left, lhs, rhs,
):
    here = coil[0]
    pieces = (p0, p1, p2, p3)
    outs = (o0, o1, o2, o3)
    for a in range(4):
        @pl.when(here == a)
        def _():
            for q in range(4):
                rows[q] = pieces[(a - q) % 4][...]
    for part, cosine, sine in ((0, ch, sh), (1, cl, sl)):
        right[part, :256, :256] = cosine[...]
        right[part, :256, 256:] = -sine[...]
        right[part, 256:, :256] = sine[...]
        right[part, 256:, 256:] = cosine[...]
    for part, cosine, sine in ((0, yh, zh), (1, yl, zl), (2, uh, wh), (3, ul, wl)):
        left[part, :256, :256] = cosine[...]
        left[part, :256, 256:] = sine[...]
        left[part, 256:, :256] = -sine[...]
        left[part, 256:, 256:] = cosine[...]

    def halves(load):
        return jnp.concatenate(
            [
                jnp.concatenate([load(y, h) for h in range(2)], axis=1)
                for y in range(4)
            ],
            axis=0,
        )

    def map_of(part, c):
        return halves(
            lambda y, h: maps[pl.ds((y * 4 + part * 2 + c) * 2 + h, 64, stride=40), :]
        )

    def image_of(part):
        return halves(lambda y, h: rows[y, pl.ds(part * 2 + h, 64, stride=4), :])

    def transform(pairs, side):
        for c in range(2):
            for part in range(2):
                high, low = split(pairs[c][part])
                lhs[0, c * 256 : c * 256 + 256, part * 256 : part * 256 + 256] = high
                lhs[1, c * 256 : c * 256 + 256, part * 256 : part * 256 + 256] = low
        for c in range(2):
            block = slice(c * 256, c * 256 + 256)
            value = (
                jnp.dot(lhs[0, block], right[0], preferred_element_type=F32)
                + jnp.dot(lhs[1, block], right[0], preferred_element_type=F32)
                + jnp.dot(lhs[0, block], right[1], preferred_element_type=F32)
            )
            for part in range(2):
                high, low = split(value[:, part * 256 : part * 256 + 256])
                rhs[0, part * 256 : part * 256 + 256, block] = high
                rhs[1, part * 256 : part * 256 + 256, block] = low
        out = []
        for part in range(2):
            block = slice(part * 256, part * 256 + 256)
            out.append(
                jnp.dot(left[side, block], rhs[0], preferred_element_type=F32)
                + jnp.dot(left[side, block], rhs[1], preferred_element_type=F32)
                + jnp.dot(left[side + 1, block], rhs[0], preferred_element_type=F32)
            )
        return [
            [out[part][:, c * 256 : c * 256 + 256] for part in range(2)]
            for c in range(2)
        ]

    vr, vi = image_of(0), image_of(1)
    pairs = []
    for c in range(2):
        sr, si = map_of(0, c), map_of(1, c)
        pairs.append([sr * vr - si * vi, sr * vi + si * vr])
    pairs = transform(pairs, 0)
    keep = mask[...].astype(F32)

    pairs = [
        [
            (pairs[c][0] - kspace[0, c]) * keep,
            (kspace[1, c] - pairs[c][1]) * keep,
        ]
        for c in range(2)
    ]
    pairs = transform(pairs, 2)
    back_re = 0.0
    back_im = 0.0
    for c in range(2):
        sr, si = map_of(0, c), map_of(1, c)
        xr, xi = pairs[c][0], -pairs[c][1]
        back_re = back_re + sr * xr + si * xi
        back_im = back_im + sr * xi - si * xr
    back = (back_re, back_im)
    for a in range(4):
        @pl.when(here == a)
        def _():
            for j in range(4):
                q = (a + j) % 4
                for part in range(2):
                    for h in range(2):
                        outs[j][pl.ds(part * 2 + h, 64, stride=4), :] = back[part][
                            q * 64 : q * 64 + 64, h * 128 : h * 128 + 128
                        ]


def transform_call(coil, maps, pieces, kspace, mask):
    vm = pl.BlockSpec(memory_space=pltpu.VMEM)
    consts = tables()
    return pl.pallas_call(
        transform_kernel,
        out_shape=tuple(jax.ShapeDtypeStruct((256, 128), F32) for _ in range(4)),
        in_specs=[pl.BlockSpec(memory_space=pltpu.SMEM)] + [vm] * 19,
        out_specs=(vm,) * 4,
        scratch_shapes=[
            pltpu.VMEM((4, 256, 128), F32),
            pltpu.VMEM((2, 512, 512), BF),
            pltpu.VMEM((4, 512, 512), BF),
            pltpu.VMEM((2, 512, 512), BF),
            pltpu.VMEM((2, 512, 512), BF),
        ],
        cost_estimate=pl.CostEstimate(
            flops=6000000000, bytes_accessed=5000000, transcendentals=0
        ),
    )(coil, maps, *pieces, kspace, mask, *[jnp.asarray(t) for t in consts])


def halos(state, grad, slab_count):
    up = [(i, i + 1) for i in range(slab_count - 1)]
    down = [(i + 1, i) for i in range(slab_count - 1)]
    high = jnp.concatenate([state[:, :, 2:], grad[:, :, 3:]], axis=2)
    low = jnp.concatenate([state[:, :, :2], grad[:, :, :1]], axis=2)
    before = lax.ppermute(high, "slab", up)
    after = lax.ppermute(low, "slab", down)

    def planes(at, last):
        rows = jnp.concatenate(
            [before[:, at, :2], state[:, at], after[:, at, :2]], axis=2
        ).reshape(4, 8, 256)
        edge = jnp.concatenate(
            [before[:, last, 2:], grad[:, last], after[:, last, 2:]], axis=1
        )
        return jnp.concatenate([rows, jnp.pad(edge, ((0, 0), (0, 2), (0, 0)))], axis=0)

    up = [(i, i + 1) for i in range(3)]
    down = [(i + 1, i) for i in range(3)]
    lower = lax.ppermute(planes(slice(14, 16), 15), "coil", up)
    upper = lax.ppermute(planes(slice(0, 2), 0), "coil", down)
    return before, after, lower, upper


def on_device(init_image, sens, kspace, mask, weights, step_sizes, recon_cotangent):
    slab_count = lax.axis_size("slab")
    coil = lax.axis_index("coil")
    slab = lax.axis_index("slab")
    maps = sens.transpose(2, 3, 0, 1, 4).reshape(64, 16, 2, 128)
    images = jnp.stack([init_image, recon_cotangent]).transpose(3, 2, 0, 1, 4)
    payload = jnp.concatenate([maps, images.reshape(64, 4, 2, 128)], axis=1)
    received = lax.all_to_all(payload, "slab", split_axis=0, concat_axis=0, tiled=True)

    before, after, lower, upper = halos(init_image, recon_cotangent, slab_count)
    wide, turned = filter_tables(weights)
    edge = jnp.stack([slab > 0, slab < slab_count - 1, coil > 0, coil < 3]).astype(F32)
    base, sums = conv_call(
        edge, init_image, recon_cotangent, before, after, lower, upper, wide, turned
    )
    partial = jnp.pad(-diagonal(sums).reshape(2592), (0, 224)).reshape(256, 11)
    chunk = jnp.sum(
        lax.all_to_all(partial, AXES, split_axis=0, concat_axis=0, tiled=True), axis=0
    )

    state_rows = received[:, 16:18].reshape(256, 128)
    grad_rows = received[:, 18:20].reshape(256, 128)
    pieces = [lax.ppermute(state_rows, AXES, spread_pairs(turn)) for turn in range(4)]
    parts = transform_call(
        coil.reshape(1), received.reshape(2560, 128), pieces, kspace[:, :, 0], mask
    )
    total = sum(
        lax.ppermute(parts[turn], AXES, return_pairs(turn)) for turn in range(4)
    )
    product = jnp.sum(total * grad_rows)
    rider = jnp.concatenate([chunk, -product[None], jnp.zeros((244,), F32)])
    rider = jnp.broadcast_to(rider.reshape(1, 1, 2, 128), (64, 1, 2, 128))
    sent = jnp.concatenate([total.reshape(64, 2, 2, 128), rider], axis=1)
    arrived = lax.all_to_all(sent, "slab", split_axis=0, concat_axis=0, tiled=True)
    combined = arrived[:, :2].reshape(4, 16, 2, 256).transpose(2, 1, 0, 3)
    recon = base - step_sizes[0] * combined
    riders = arrived[:, 2, 0, :12]
    small = jnp.concatenate([riders[:, :11].reshape(704), jnp.sum(riders[:, 11])[None]])
    small = jnp.pad(small, (0, 319)).reshape(8, 128)
    others = [small] + [
        lax.ppermute(small, "coil", [(i, (i + turn) % 4) for i in range(4)])
        for turn in range(1, 4)
    ]
    reverse = jnp.stack([others[0], others[3], others[2], others[1]])
    ordered = rotated(reverse, (4 - coil) % 4).reshape(4, 1024)
    step_grads = jnp.sum(ordered[:, 704])[None]
    grads = ordered[:, :704].reshape(4, 64, 11).transpose(1, 0, 2).reshape(2816)[:2592]
    grads = grads.reshape(3, 3, 2, 3, 48).transpose(4, 2, 1, 3, 0)
    return recon, grads[None], step_grads


def solution(mesh):
    return jax.shard_map(
        on_device,
        mesh=mesh,
        in_specs=(
            P(None, "coil", "slab", None),
            P(None, "coil", None, "slab", None),
            P(None, "coil", "slab", None, None),
            P(),
            P(),
            P(),
            P(None, "coil", "slab", None),
        ),
        out_specs=(P(None, "coil", "slab", None), P(), P()),
        check_vma=False,
    )
```

```python
import jax
import jax.numpy as jnp
import numpy as np
from jax import lax
from jax.experimental import pallas as pl
from jax.experimental.pallas import tpu as pltpu
from jax.sharding import PartitionSpec as P

AXES = ("slab", "coil")
BF = jnp.bfloat16
F32 = jnp.float32


def holder(coil, quarter, low):
    z = (low // 4 - 1 + 2 * (coil % 2)) % 4 * 2 + quarter % 2
    return (quarter // 2 * 32 + z * 4 + low % 4) * 4 + coil


def reader(coil, group, low):
    return (group * 16 + low) * 4 + coil


def spread_pairs(turn):
    return [
        (holder(c, q, low), reader((q + turn) % 4, c, low))
        for c in range(4)
        for q in range(4)
        for low in range(16)
    ]


def return_pairs(turn):
    return [
        (reader(c, b, low), holder(b, (c + turn) % 4, low))
        for c in range(4)
        for b in range(4)
        for low in range(16)
    ]


def turned_by_core(data, coil, axis, sign):
    even = jnp.roll(data, sign, axis)
    odd = jnp.roll(data, -sign, axis)
    return jnp.where(coil % 2 == 0, even, odd)


def split(value):
    high = value.astype(BF)
    return high, (value - high.astype(F32)).astype(BF)


def split_outside(value):
    high = lax.reduce_precision(value, 8, 7)
    return high.astype(BF), (value - high).astype(BF)


def shifted(value, step):
    if step == 0:
        return value
    lane = lax.broadcasted_iota(jnp.int32, value.shape, value.ndim - 1)
    turned = pltpu.roll(value, step % 256, value.ndim - 1)
    edge = 0 if step > 0 else 255
    return jnp.where(lane == edge, 0.0, turned)


def filter_tables(weights):
    taps = np.zeros((3, 6, 8), np.float32)
    for d in range(3):
        for y in range(6):
            taps[d, y, y + d] = 1.0
    kernel = weights[0]
    ahead = sum(
        kernel[:, :, :, d][:, :, :, :, None, None] * taps[d] for d in range(3)
    )
    ahead = ahead.transpose(4, 0, 3, 2, 1, 5).reshape(288, 144)
    back = np.zeros((3, 4, 6), np.float32)
    for d in range(3):
        for y in range(4):
            back[d, y, y + 2 - d] = 1.0
    behind = sum(
        kernel[:, :, :, d][:, :, :, :, None, None] * back[d] for d in range(3)
    )
    behind = behind.transpose(2, 3, 1, 4, 5, 0).reshape(72, 288)
    high, low = split_outside(ahead)
    wide = jnp.concatenate([high, low, high], axis=1)
    high, low = split_outside(behind)
    turned = jnp.concatenate(
        [
            jnp.concatenate([high, high], axis=1),
            jnp.concatenate([low, jnp.zeros_like(low)], axis=1),
        ],
        axis=0,
    )
    return wide, turned


def conv_kernel(
    edge, init, grad, before, after, lower, upper, wide, turned, base, sums,
    xs, gs, xb, gb, acc,
):
    gs[:, :, 0:1] = jnp.zeros((18, 2, 1, 256), F32)
    gs[:, :, 7:8] = jnp.zeros((18, 2, 1, 256), F32)
    for i in range(2):
        xs[2:18, i, 2:6] = init[i]
        xs[2:18, i, 0:2] = before[i, :, 0:2]
        xs[2:18, i, 6:8] = after[i, :, 0:2]
        xs[0:2, i] = lower[2 * i : 2 * i + 2]
        xs[18:20, i] = upper[2 * i : 2 * i + 2]
        gs[1:17, i, 2:6] = grad[i]
        gs[1:17, i, 1:2] = before[i, :, 2:3]
        gs[1:17, i, 6:7] = after[i, :, 2:3]
        gs[0:1, i, 1:7] = lower[4 + i : 5 + i, 0:6]
        gs[17:18, i, 1:7] = upper[4 + i : 5 + i, 0:6]
    for plain, packed, count in ((xs, xb, 320), (gs, gb, 288)):
        value = plain[...].reshape(count, 256)
        for d in range(3):
            high, low = split(shifted(value, 1 - d))
            packed[d, 0] = high
            packed[d, 1] = low
    acc[...] = jnp.zeros_like(acc)
    sums[...] = jnp.zeros_like(sums)
    row = lax.broadcasted_iota(jnp.int32, (288, 256), 0)
    keep = jnp.where(row < 48, edge[0], jnp.where(row >= 240, edge[1], 1.0))

    def window(packed, place, part):
        start = pl.multiple_of(place * 16, 16)
        return jnp.concatenate(
            [packed[d, part, pl.ds(start, 48)] for d in range(3)], axis=0
        )

    def forward(place, table, packed):
        high = window(packed, place, 0)
        low = window(packed, place, 1)
        data = jnp.concatenate([high, high, low], axis=0)
        return jnp.dot(table, data, preferred_element_type=F32), high, low

    def scatter(place, high, low):
        data = jnp.concatenate([high, low], axis=0)
        product = jnp.dot(turned[...], data, preferred_element_type=F32)
        product = product[:72] + product[72:]
        for r in range(3):
            for d in range(3):
                first = (r * 3 + d) * 8
                acc[d, pl.ds(place + r, 1)] += product[first : first + 8][None]

    def border(k, carry):
        place = 17 * k
        scale = jnp.where(k == 0, edge[2], edge[3])
        response, _, _ = forward(place, wide[...], xb)
        high, low = split(jnp.tanh(response) * (keep * scale))
        scatter(place, high, low)
        return carry

    def step(r, carry):
        response, xh, xl = forward(r + 1, wide[...], xb)
        linear, gh, gl = forward(r, wide[48:240], gb)
        active = jnp.tanh(response) * keep
        core = active[48:240]
        weighted = (1.0 - core * core) * linear
        high, low = split(active)
        wh, wl = split(weighted)
        ch, cl = high[48:240], low[48:240]
        left = jnp.concatenate([gh, gh, gl, xh, xh, xl], axis=1)
        right = jnp.concatenate([ch, cl, ch, wh, wl, wh], axis=1)
        sums[...] += lax.dot_general(
            left, right, (((1,), (1,)), ((), ())), preferred_element_type=F32
        )
        scatter(r + 1, high, low)
        return carry

    lax.fori_loop(0, 2, border, 0)
    lax.fori_loop(0, 16, step, 0)
    total = (
        shifted(acc[0, 2:18].reshape(128, 256), -1)
        + acc[1, 2:18].reshape(128, 256)
        + shifted(acc[2, 2:18].reshape(128, 256), 1)
    ).reshape(16, 8, 256)
    for i in range(2):
        base[i] = init[i] - total[:, 4 * i : 4 * i + 4]


def conv_call(edge, init, grad, before, after, lower, upper, wide, turned):
    vm = pl.BlockSpec(memory_space=pltpu.VMEM)
    return pl.pallas_call(
        conv_kernel,
        out_shape=(
            jax.ShapeDtypeStruct((2, 16, 4, 256), F32),
            jax.ShapeDtypeStruct((144, 192), F32),
        ),
        in_specs=[pl.BlockSpec(memory_space=pltpu.SMEM)] + [vm] * 8,
        out_specs=(vm, vm),
        scratch_shapes=[
            pltpu.VMEM((20, 2, 8, 256), F32),
            pltpu.VMEM((18, 2, 8, 256), F32),
            pltpu.VMEM((3, 2, 320, 256), BF),
            pltpu.VMEM((3, 2, 288, 256), BF),
            pltpu.VMEM((3, 20, 8, 256), F32),
        ],
        cost_estimate=pl.CostEstimate(
            flops=6000000000, bytes_accessed=2000000, transcendentals=1300000
        ),
    )(edge, init, grad, before, after, lower, upper, wide, turned)


def diagonal(sums):
    cube = sums.reshape(3, 3, 2, 8, 4, 48)
    taps = [
        sum(cube[:, :, :, y + 1 + d, y] for y in range(4)) for d in range(3)
    ]
    return jnp.stack(taps, axis=3)


def tables():
    place = np.arange(256)
    mixed = place % 64 * 4 + place // 64
    made = []
    for first, second in ((place, place), (place, mixed), (mixed, place)):
        angle = (first[:, None] * second[None, :] % 256) * (2.0 * np.pi / 256)
        for table in (np.cos(angle) / 16.0, np.sin(angle) / 16.0):
            table = np.asarray(table, np.float32)
            high = table.astype(BF)
            made.append(high)
            made.append((table - high.astype(np.float32)).astype(BF))
    return made


def transform_kernel(
    coil, maps, p0, p1, p2, p3, kspace, mask, ch, cl, sh, sl, yh, yl, zh, zl,
    uh, ul, wh, wl, o0, o1, o2, o3, rows, right, left, lhs, rhs,
):
    here = coil[0]
    pieces = (p0, p1, p2, p3)
    outs = (o0, o1, o2, o3)
    for a in range(4):
        @pl.when(here == a)
        def _():
            for q in range(4):
                rows[q] = pieces[(a - q) % 4][...]
    for part, cosine, sine in ((0, ch, sh), (1, cl, sl)):
        right[part, :256, :256] = cosine[...]
        right[part, :256, 256:] = -sine[...]
        right[part, 256:, :256] = sine[...]
        right[part, 256:, 256:] = cosine[...]
    for part, cosine, sine in ((0, yh, zh), (1, yl, zl), (2, uh, wh), (3, ul, wl)):
        left[part, :256, :256] = cosine[...]
        left[part, :256, 256:] = sine[...]
        left[part, 256:, :256] = -sine[...]
        left[part, 256:, 256:] = cosine[...]

    def halves(load):
        return jnp.concatenate(
            [
                jnp.concatenate([load(y, h) for h in range(2)], axis=1)
                for y in range(4)
            ],
            axis=0,
        )

    def map_of(part, c):
        return halves(
            lambda y, h: maps[pl.ds((y * 4 + part * 2 + c) * 2 + h, 64, stride=40), :]
        )

    def image_of(part):
        return halves(lambda y, h: rows[y, pl.ds(part * 2 + h, 64, stride=4), :])

    def transform(pairs, side):
        for c in range(2):
            for part in range(2):
                high, low = split(pairs[c][part])
                lhs[0, c * 256 : c * 256 + 256, part * 256 : part * 256 + 256] = high
                lhs[1, c * 256 : c * 256 + 256, part * 256 : part * 256 + 256] = low
        for c in range(2):
            block = slice(c * 256, c * 256 + 256)
            value = (
                jnp.dot(lhs[0, block], right[0], preferred_element_type=F32)
                + jnp.dot(lhs[1, block], right[0], preferred_element_type=F32)
                + jnp.dot(lhs[0, block], right[1], preferred_element_type=F32)
            )
            for part in range(2):
                high, low = split(value[:, part * 256 : part * 256 + 256])
                rhs[0, part * 256 : part * 256 + 256, block] = high
                rhs[1, part * 256 : part * 256 + 256, block] = low
        out = []
        for part in range(2):
            block = slice(part * 256, part * 256 + 256)
            out.append(
                jnp.dot(left[side, block], rhs[0], preferred_element_type=F32)
                + jnp.dot(left[side, block], rhs[1], preferred_element_type=F32)
                + jnp.dot(left[side + 1, block], rhs[0], preferred_element_type=F32)
            )
        return [
            [out[part][:, c * 256 : c * 256 + 256] for part in range(2)]
            for c in range(2)
        ]

    vr, vi = image_of(0), image_of(1)
    pairs = []
    for c in range(2):
        sr, si = map_of(0, c), map_of(1, c)
        pairs.append([sr * vr - si * vi, sr * vi + si * vr])
    pairs = transform(pairs, 0)
    keep = mask[...].astype(F32)

    pairs = [
        [
            (pairs[c][0] - kspace[0, c]) * keep,
            (kspace[1, c] - pairs[c][1]) * keep,
        ]
        for c in range(2)
    ]
    pairs = transform(pairs, 2)
    back_re = 0.0
    back_im = 0.0
    for c in range(2):
        sr, si = map_of(0, c), map_of(1, c)
        xr, xi = pairs[c][0], -pairs[c][1]
        back_re = back_re + sr * xr + si * xi
        back_im = back_im + sr * xi - si * xr
    back = (back_re, back_im)
    for a in range(4):
        @pl.when(here == a)
        def _():
            for j in range(4):
                q = (a + j) % 4
                for part in range(2):
                    for h in range(2):
                        outs[j][pl.ds(part * 2 + h, 64, stride=4), :] = back[part][
                            q * 64 : q * 64 + 64, h * 128 : h * 128 + 128
                        ]


def transform_call(coil, maps, pieces, kspace, mask):
    vm = pl.BlockSpec(memory_space=pltpu.VMEM)
    consts = tables()
    return pl.pallas_call(
        transform_kernel,
        out_shape=tuple(jax.ShapeDtypeStruct((256, 128), F32) for _ in range(4)),
        in_specs=[pl.BlockSpec(memory_space=pltpu.SMEM)] + [vm] * 19,
        out_specs=(vm,) * 4,
        scratch_shapes=[
            pltpu.VMEM((4, 256, 128), F32),
            pltpu.VMEM((2, 512, 512), BF),
            pltpu.VMEM((4, 512, 512), BF),
            pltpu.VMEM((2, 512, 512), BF),
            pltpu.VMEM((2, 512, 512), BF),
        ],
        cost_estimate=pl.CostEstimate(
            flops=6000000000, bytes_accessed=5000000, transcendentals=0
        ),
    )(coil, maps, *pieces, kspace, mask, *[jnp.asarray(t) for t in consts])


def halos(state, grad, slab_count):
    up = [(i, i + 1) for i in range(slab_count - 1)]
    down = [(i + 1, i) for i in range(slab_count - 1)]
    high = jnp.concatenate([state[:, :, 2:], grad[:, :, 3:]], axis=2)
    low = jnp.concatenate([state[:, :, :2], grad[:, :, :1]], axis=2)
    before = lax.ppermute(high, "slab", up)
    after = lax.ppermute(low, "slab", down)

    def planes(at, last):
        rows = jnp.concatenate(
            [before[:, at, :2], state[:, at], after[:, at, :2]], axis=2
        ).reshape(4, 8, 256)
        edge = jnp.concatenate(
            [before[:, last, 2:], grad[:, last], after[:, last, 2:]], axis=1
        )
        return jnp.concatenate([rows, jnp.pad(edge, ((0, 0), (0, 2), (0, 0)))], axis=0)

    up = [(i, i + 1) for i in range(3)]
    down = [(i + 1, i) for i in range(3)]
    lower = lax.ppermute(planes(slice(14, 16), 15), "coil", up)
    upper = lax.ppermute(planes(slice(0, 2), 0), "coil", down)
    return before, after, lower, upper


def on_device(init_image, sens, kspace, mask, weights, step_sizes, recon_cotangent):
    slab_count = lax.axis_size("slab")
    coil = lax.axis_index("coil")
    slab = lax.axis_index("slab")
    maps = sens.transpose(2, 3, 0, 1, 4).reshape(64, 16, 2, 128)
    images = jnp.stack([init_image, recon_cotangent]).reshape(2, 2, 4, 4, 2, 2, 256)
    images = images.transpose(4, 2, 5, 3, 0, 1, 6)
    images = turned_by_core(images, coil, 1, -1).reshape(64, 4, 2, 128)
    payload = jnp.concatenate([maps, images], axis=1)
    received = lax.all_to_all(payload, "slab", split_axis=0, concat_axis=0, tiled=True)

    before, after, lower, upper = halos(init_image, recon_cotangent, slab_count)
    wide, turned = filter_tables(weights)
    edge = jnp.stack([slab > 0, slab < slab_count - 1, coil > 0, coil < 3]).astype(F32)
    base, sums = conv_call(
        edge, init_image, recon_cotangent, before, after, lower, upper, wide, turned
    )
    partial = jnp.pad(-diagonal(sums).reshape(2592), (0, 32)).reshape(64, 1, 41)
    partial = jnp.broadcast_to(partial, (64, 4, 41)).reshape(256, 41)
    chunk = lax.all_to_all(partial, AXES, split_axis=0, concat_axis=0, tiled=True)
    chunk = jnp.sum(chunk, axis=0)

    state_rows = received[:, 16:18].reshape(256, 128)
    grad_rows = received[:, 18:20].reshape(256, 128)
    pieces = [lax.ppermute(state_rows, AXES, spread_pairs(turn)) for turn in range(4)]
    parts = transform_call(
        coil.reshape(1), received.reshape(2560, 128), pieces, kspace[:, :, 0], mask
    )
    total = sum(
        lax.ppermute(parts[turn], AXES, return_pairs(turn)) for turn in range(4)
    )
    product = jnp.sum(total * grad_rows)
    rider = jnp.concatenate([chunk, -product[None], jnp.zeros((214,), F32)])
    rider = jnp.broadcast_to(rider.reshape(1, 1, 2, 128), (64, 1, 2, 128))
    sent = jnp.concatenate([total.reshape(64, 2, 2, 128), rider], axis=1)
    arrived = lax.all_to_all(sent, "slab", split_axis=0, concat_axis=0, tiled=True)
    own = jnp.sum(arrived[:, 2, 0, 41])[None]
    step_grads = own
    for turn in range(1, 4):
        step_grads = step_grads + lax.ppermute(
            own, "coil", [(i, (i + turn) % 4) for i in range(4)]
        )
    combined = arrived[:, :2].reshape(2, 4, 2, 4, 2, 256)
    combined = turned_by_core(combined, coil, 1, 1).transpose(4, 1, 3, 0, 2, 5)
    recon = base - step_sizes[0] * combined.reshape(2, 16, 4, 256)
    grads = arrived[:, 2, 0, :41].reshape(2624)[:2592]
    grads = grads.reshape(3, 3, 2, 3, 48).transpose(4, 2, 1, 3, 0)
    return recon, grads[None], step_grads


def solution(mesh):
    return jax.shard_map(
        on_device,
        mesh=mesh,
        in_specs=(
            P(None, "coil", "slab", None),
            P(None, "coil", None, "slab", None),
            P(None, "coil", "slab", None, None),
            P(),
            P(),
            P(),
            P(None, "coil", "slab", None),
        ),
        out_specs=(P(None, "coil", "slab", None), P(), P()),
        check_vma=False,
    )
```

```python
import jax
import jax.numpy as jnp
import numpy as np
from jax import lax
from jax.experimental import pallas as pl
from jax.experimental.pallas import tpu as pltpu
from jax.sharding import PartitionSpec as P

AXES = ("slab", "coil")
BF = jnp.bfloat16
F32 = jnp.float32


def holder(coil, quarter, low):
    z = (low // 4 * 2 - 2 + 4 * (coil % 2) + low % 2) % 8
    y = low % 4 // 2 * 2 + quarter % 2
    return (quarter // 2 * 32 + z * 4 + y) * 4 + coil


def reader(coil, group, low):
    return (group * 16 + low) * 4 + coil


def far_pairs(turn):
    return [
        (holder(c, q, low), reader((q // 2 ^ turn) * 2 + q % 2, c, low))
        for c in range(4)
        for q in range(4)
        for low in range(16)
    ]


def back_pairs(turn):
    return [(to, at) for at, to in far_pairs(turn)]


CORES = [(i, i ^ 1) for i in range(4)]
GROUPS = [[x * 32 + e + 2 * k for k in range(16)] for x in range(2) for e in range(2)]


def turned_by_core(data, coil, axis, sign):
    even = jnp.roll(data, sign, axis)
    odd = jnp.roll(data, -sign, axis)
    return jnp.where(coil % 2 == 0, even, odd)


def split(value):
    high = value.astype(BF)
    return high, (value - high.astype(F32)).astype(BF)


def split_outside(value):
    high = lax.reduce_precision(value, 8, 7)
    return high.astype(BF), (value - high).astype(BF)


def shifted(value, step):
    if step == 0:
        return value
    lane = lax.broadcasted_iota(jnp.int32, value.shape, value.ndim - 1)
    turned = pltpu.roll(value, step % 256, value.ndim - 1)
    edge = 0 if step > 0 else 255
    return jnp.where(lane == edge, 0.0, turned)


def filter_tables(weights):
    taps = np.zeros((3, 6, 8), np.float32)
    for d in range(3):
        for y in range(6):
            taps[d, y, y + d] = 1.0
    kernel = weights[0]
    ahead = sum(
        kernel[:, :, :, d][:, :, :, :, None, None] * taps[d] for d in range(3)
    )
    ahead = ahead.transpose(4, 0, 3, 2, 1, 5).reshape(288, 144)
    back = np.zeros((3, 4, 6), np.float32)
    for d in range(3):
        for y in range(4):
            back[d, y, y + 2 - d] = 1.0
    behind = sum(
        kernel[:, :, :, d][:, :, :, :, None, None] * back[d] for d in range(3)
    )
    behind = behind.transpose(2, 3, 1, 4, 5, 0).reshape(72, 288)
    high, low = split_outside(ahead)
    wide = jnp.concatenate([high, low, high], axis=1)
    high, low = split_outside(behind)
    turned = jnp.concatenate(
        [
            jnp.concatenate([high, high], axis=1),
            jnp.concatenate([low, jnp.zeros_like(low)], axis=1),
        ],
        axis=0,
    )
    return wide, turned


def conv_kernel(
    edge, init, grad, before, after, lower, upper, wide, turned, base, sums,
    xs, gs, xb, gb, acc,
):
    gs[:, :, 0:1] = jnp.zeros((18, 2, 1, 256), F32)
    gs[:, :, 7:8] = jnp.zeros((18, 2, 1, 256), F32)
    for i in range(2):
        xs[2:18, i, 2:6] = init[i]
        xs[2:18, i, 0:2] = before[i, :, 0:2]
        xs[2:18, i, 6:8] = after[i, :, 0:2]
        xs[0:2, i] = lower[2 * i : 2 * i + 2]
        xs[18:20, i] = upper[2 * i : 2 * i + 2]
        gs[1:17, i, 2:6] = grad[i]
        gs[1:17, i, 1:2] = before[i, :, 2:3]
        gs[1:17, i, 6:7] = after[i, :, 2:3]
        gs[0:1, i, 1:7] = lower[4 + i : 5 + i, 0:6]
        gs[17:18, i, 1:7] = upper[4 + i : 5 + i, 0:6]
    for plain, packed, count in ((xs, xb, 320), (gs, gb, 288)):
        value = plain[...].reshape(count, 256)
        for d in range(3):
            high, low = split(shifted(value, 1 - d))
            packed[d, 0] = high
            packed[d, 1] = low
    acc[...] = jnp.zeros_like(acc)
    sums[...] = jnp.zeros_like(sums)
    row = lax.broadcasted_iota(jnp.int32, (288, 256), 0)
    keep = jnp.where(row < 48, edge[0], jnp.where(row >= 240, edge[1], 1.0))

    def window(packed, place, part):
        start = pl.multiple_of(place * 16, 16)
        return jnp.concatenate(
            [packed[d, part, pl.ds(start, 48)] for d in range(3)], axis=0
        )

    def forward(place, table, packed):
        high = window(packed, place, 0)
        low = window(packed, place, 1)
        data = jnp.concatenate([high, high, low], axis=0)
        return jnp.dot(table, data, preferred_element_type=F32), high, low

    def scatter(place, high, low):
        data = jnp.concatenate([high, low], axis=0)
        product = jnp.dot(turned[...], data, preferred_element_type=F32)
        product = product[:72] + product[72:]
        for r in range(3):
            for d in range(3):
                first = (r * 3 + d) * 8
                acc[d, pl.ds(place + r, 1)] += product[first : first + 8][None]

    def border(k, carry):
        place = 17 * k
        scale = jnp.where(k == 0, edge[2], edge[3])
        response, _, _ = forward(place, wide[...], xb)
        high, low = split(jnp.tanh(response) * (keep * scale))
        scatter(place, high, low)
        return carry

    def step(r, carry):
        response, xh, xl = forward(r + 1, wide[...], xb)
        linear, gh, gl = forward(r, wide[48:240], gb)
        active = jnp.tanh(response) * keep
        core = active[48:240]
        weighted = (1.0 - core * core) * linear
        high, low = split(active)
        wh, wl = split(weighted)
        ch, cl = high[48:240], low[48:240]
        left = jnp.concatenate([gh, gh, gl, xh, xh, xl], axis=1)
        right = jnp.concatenate([ch, cl, ch, wh, wl, wh], axis=1)
        sums[...] += lax.dot_general(
            left, right, (((1,), (1,)), ((), ())), preferred_element_type=F32
        )
        scatter(r + 1, high, low)
        return carry

    lax.fori_loop(0, 2, border, 0)
    lax.fori_loop(0, 16, step, 0)
    total = (
        shifted(acc[0, 2:18].reshape(128, 256), -1)
        + acc[1, 2:18].reshape(128, 256)
        + shifted(acc[2, 2:18].reshape(128, 256), 1)
    ).reshape(16, 8, 256)
    for i in range(2):
        base[i] = init[i] - total[:, 4 * i : 4 * i + 4]


def conv_call(edge, init, grad, before, after, lower, upper, wide, turned):
    vm = pl.BlockSpec(memory_space=pltpu.VMEM)
    return pl.pallas_call(
        conv_kernel,
        out_shape=(
            jax.ShapeDtypeStruct((2, 16, 4, 256), F32),
            jax.ShapeDtypeStruct((144, 192), F32),
        ),
        in_specs=[pl.BlockSpec(memory_space=pltpu.SMEM)] + [vm] * 8,
        out_specs=(vm, vm),
        scratch_shapes=[
            pltpu.VMEM((20, 2, 8, 256), F32),
            pltpu.VMEM((18, 2, 8, 256), F32),
            pltpu.VMEM((3, 2, 320, 256), BF),
            pltpu.VMEM((3, 2, 288, 256), BF),
            pltpu.VMEM((3, 20, 8, 256), F32),
        ],
        cost_estimate=pl.CostEstimate(
            flops=6000000000, bytes_accessed=2000000, transcendentals=1300000
        ),
    )(edge, init, grad, before, after, lower, upper, wide, turned)


def diagonal(sums):
    cube = sums.reshape(3, 3, 2, 8, 4, 48)
    taps = [
        sum(cube[:, :, :, y + 1 + d, y] for y in range(4)) for d in range(3)
    ]
    return jnp.stack(taps, axis=3)


def tables():
    place = np.arange(256)
    mixed = (place // 128 * 32 + place // 64 % 2 + place % 16 * 2) * 4
    mixed = mixed + place // 16 % 4
    made = []
    for first, second in ((place, place), (place, mixed), (mixed, place)):
        angle = (first[:, None] * second[None, :] % 256) * (2.0 * np.pi / 256)
        for table in (np.cos(angle) / 16.0, np.sin(angle) / 16.0):
            table = np.asarray(table, np.float32)
            high = table.astype(BF)
            made.append(high)
            made.append((table - high.astype(np.float32)).astype(BF))
    return made


def transform_kernel(
    coil, maps, p0, p1, p2, p3, kspace, mask, extra, ch, cl, sh, sl, yh, yl, zh, zl,
    uh, ul, wh, wl, kept, sent, rows, right, left, lhs, rhs,
):
    here = coil[0]
    pieces = (p0, p1, p2, p3)

    def slot(a, q):
        return (q // 2 ^ a // 2) + 2 * (q % 2 ^ a % 2)

    for a in range(4):
        @pl.when(here == a)
        def _():
            for q in range(4):
                rows[q] = pieces[slot(a, q)][...]
    for part, cosine, sine in ((0, ch, sh), (1, cl, sl)):
        right[part, :256, :256] = cosine[...]
        right[part, :256, 256:] = -sine[...]
        right[part, 256:, :256] = sine[...]
        right[part, 256:, 256:] = cosine[...]
    for part, cosine, sine in ((0, yh, zh), (1, yl, zl), (2, uh, wh), (3, ul, wl)):
        left[part, :256, :256] = cosine[...]
        left[part, :256, 256:] = sine[...]
        left[part, 256:, :256] = -sine[...]
        left[part, 256:, 256:] = cosine[...]

    def halves(load):
        return jnp.concatenate(
            [
                jnp.concatenate([load(q, y, h) for h in range(2)], axis=1)
                for q in range(4)
                for y in range(4)
            ],
            axis=0,
        )

    def map_of(part, c):
        def load(q, y, h):
            first = (q // 2 * 32 + q % 2) * 32 + (y * 4 + part * 2 + c) * 2 + h
            return maps[pl.ds(first, 16, stride=64), :]

        return halves(load)

    def image_of(which, part):
        def load(q, y, h):
            return rows[q, pl.ds((which * 8 + part * 4 + y) * 2 + h, 16, stride=32), :]

        return halves(load)

    def transform(pairs, side):
        for c in range(2):
            for part in range(2):
                high, low = split(pairs[c][part])
                lhs[0, c * 256 : c * 256 + 256, part * 256 : part * 256 + 256] = high
                lhs[1, c * 256 : c * 256 + 256, part * 256 : part * 256 + 256] = low
        for c in range(2):
            block = slice(c * 256, c * 256 + 256)
            value = (
                jnp.dot(lhs[0, block], right[0], preferred_element_type=F32)
                + jnp.dot(lhs[1, block], right[0], preferred_element_type=F32)
                + jnp.dot(lhs[0, block], right[1], preferred_element_type=F32)
            )
            for part in range(2):
                high, low = split(value[:, part * 256 : part * 256 + 256])
                rhs[0, part * 256 : part * 256 + 256, block] = high
                rhs[1, part * 256 : part * 256 + 256, block] = low
        out = []
        for part in range(2):
            block = slice(part * 256, part * 256 + 256)
            out.append(
                jnp.dot(left[side, block], rhs[0], preferred_element_type=F32)
                + jnp.dot(left[side, block], rhs[1], preferred_element_type=F32)
                + jnp.dot(left[side + 1, block], rhs[0], preferred_element_type=F32)
            )
        return [
            [out[part][:, c * 256 : c * 256 + 256] for part in range(2)]
            for c in range(2)
        ]

    vr, vi = image_of(0, 0), image_of(0, 1)
    pairs = []
    for c in range(2):
        sr, si = map_of(0, c), map_of(1, c)
        pairs.append([sr * vr - si * vi, sr * vi + si * vr])
    pairs = transform(pairs, 0)
    keep = mask[...].astype(F32)

    pairs = [
        [
            (pairs[c][0] - kspace[0, c]) * keep,
            (kspace[1, c] - pairs[c][1]) * keep,
        ]
        for c in range(2)
    ]
    pairs = transform(pairs, 2)
    back_re = 0.0
    back_im = 0.0
    for c in range(2):
        sr, si = map_of(0, c), map_of(1, c)
        xr, xi = pairs[c][0], -pairs[c][1]
        back_re = back_re + sr * xr + si * xi
        back_im = back_im + sr * xi - si * xr
    back = (back_re, back_im)
    product = jnp.sum(
        back_re * image_of(1, 0) + back_im * image_of(1, 1), axis=0, keepdims=True
    )
    product = product[:, :128] + product[:, 128:]
    for out in (kept, sent):
        for t in range(2):
            out[t, 256:280] = extra[...]
            out[t, 278:279] = -product
    for a in range(4):
        @pl.when(here == a)
        def _():
            for q in range(4):
                place = slot(a, q)
                out = sent if place >= 2 else kept
                for part in range(2):
                    for y in range(4):
                        for h in range(2):
                            first = (part * 4 + y) * 2 + h
                            out[place % 2, pl.ds(first, 16, stride=16), :] = back[part][
                                q * 64 + y * 16 : q * 64 + y * 16 + 16,
                                h * 128 : h * 128 + 128,
                            ]


def transform_call(coil, maps, pieces, kspace, mask, extra):
    vm = pl.BlockSpec(memory_space=pltpu.VMEM)
    consts = tables()
    return pl.pallas_call(
        transform_kernel,
        out_shape=tuple(jax.ShapeDtypeStruct((2, 280, 128), F32) for _ in range(2)),
        in_specs=[pl.BlockSpec(memory_space=pltpu.SMEM)] + [vm] * 20,
        out_specs=(vm,) * 2,
        scratch_shapes=[
            pltpu.VMEM((4, 512, 128), F32),
            pltpu.VMEM((2, 512, 512), BF),
            pltpu.VMEM((4, 512, 512), BF),
            pltpu.VMEM((2, 512, 512), BF),
            pltpu.VMEM((2, 512, 512), BF),
        ],
        cost_estimate=pl.CostEstimate(
            flops=6000000000, bytes_accessed=5000000, transcendentals=0
        ),
    )(coil, maps, *pieces, kspace, mask, extra, *[jnp.asarray(t) for t in consts])


def halos(state, grad, slab_count):
    up = [(i, i + 1) for i in range(slab_count - 1)]
    down = [(i + 1, i) for i in range(slab_count - 1)]
    high = jnp.concatenate([state[:, :, 2:], grad[:, :, 3:]], axis=2)
    low = jnp.concatenate([state[:, :, :2], grad[:, :, :1]], axis=2)
    before = lax.ppermute(high, "slab", up)
    after = lax.ppermute(low, "slab", down)

    def planes(at, last):
        rows = jnp.concatenate(
            [before[:, at, :2], state[:, at], after[:, at, :2]], axis=2
        ).reshape(4, 8, 256)
        edge = jnp.concatenate(
            [before[:, last, 2:], grad[:, last], after[:, last, 2:]], axis=1
        )
        return jnp.concatenate([rows, jnp.pad(edge, ((0, 0), (0, 2), (0, 0)))], axis=0)

    up = [(i, i + 1) for i in range(3)]
    down = [(i + 1, i) for i in range(3)]
    lower = lax.ppermute(planes(slice(14, 16), 15), "coil", up)
    upper = lax.ppermute(planes(slice(0, 2), 0), "coil", down)
    return before, after, lower, upper


def on_device(init_image, sens, kspace, mask, weights, step_sizes, recon_cotangent):
    slab_count = lax.axis_size("slab")
    coil = lax.axis_index("coil")
    slab = lax.axis_index("slab")
    images = jnp.stack([init_image, recon_cotangent]).reshape(2, 2, 4, 2, 2, 4, 256)
    images = images.transpose(2, 4, 3, 0, 1, 5, 6)
    images = turned_by_core(images, coil, 0, -1).reshape(16, 32, 128)
    images = lax.all_to_all(
        images, "slab", split_axis=0, concat_axis=0, tiled=True,
        axis_index_groups=GROUPS,
    )
    maps = sens.transpose(2, 3, 0, 1, 4).reshape(64, 32, 128)
    maps, images = lax.optimization_barrier((maps, images))
    received = lax.all_to_all(maps, "slab", split_axis=0, concat_axis=0, tiled=True)

    before, after, lower, upper = halos(init_image, recon_cotangent, slab_count)
    wide, turned = filter_tables(weights)
    edge = jnp.stack([slab > 0, slab < slab_count - 1, coil > 0, coil < 3]).astype(F32)
    base, sums = conv_call(
        edge, init_image, recon_cotangent, before, after, lower, upper, wide, turned
    )
    extra = jnp.pad(-diagonal(sums).reshape(2592), (0, 480)).reshape(24, 128)

    held = images.reshape(512, 128)
    pieces = [lax.ppermute(held, AXES, far_pairs(turn)) for turn in range(2)]
    pieces = pieces + [lax.ppermute(piece, "coil", CORES) for piece in pieces]
    kept, sent = transform_call(
        coil.reshape(1), received.reshape(2048, 128), pieces, kspace[:, :, 0], mask,
        extra,
    )
    kept = kept + lax.ppermute(sent, "coil", CORES)
    total = lax.ppermute(kept[0], AXES, back_pairs(0)) + lax.ppermute(
        kept[1], AXES, back_pairs(1)
    )
    rider = jnp.broadcast_to(total[None, 256:], (16, 24, 128))
    sent = jnp.concatenate([total[:256].reshape(16, 16, 128), rider], axis=1)
    arrived = lax.all_to_all(
        sent, "slab", split_axis=0, concat_axis=0, tiled=True,
        axis_index_groups=GROUPS,
    )
    own = jnp.sum(arrived[:, 16:], axis=0)
    riders = own
    for turn in range(1, 4):
        riders = riders + lax.ppermute(
            own, "coil", [(i, (i + turn) % 4) for i in range(4)]
        )
    combined = arrived[:, :16].reshape(4, 2, 2, 2, 4, 256)
    combined = turned_by_core(combined, coil, 0, 1).transpose(3, 0, 2, 1, 4, 5)
    recon = base - step_sizes[0] * combined.reshape(2, 16, 4, 256)
    step_grads = jnp.sum(riders[22])[None]
    grads = riders[:21].reshape(2688)[:2592]
    grads = grads.reshape(3, 3, 2, 3, 48).transpose(4, 2, 1, 3, 0)
    return recon, grads[None], step_grads


def solution(mesh):
    return jax.shard_map(
        on_device,
        mesh=mesh,
        in_specs=(
            P(None, "coil", "slab", None),
            P(None, "coil", None, "slab", None),
            P(None, "coil", "slab", None, None),
            P(),
            P(),
            P(),
            P(None, "coil", "slab", None),
        ),
        out_specs=(P(None, "coil", "slab", None), P(), P()),
        check_vma=False,
    )
```

```python
import jax
import jax.numpy as jnp
import numpy as np
from jax import lax
from jax.experimental import pallas as pl
from jax.experimental.pallas import tpu as pltpu
from jax.sharding import PartitionSpec as P

AXES = ("slab", "coil")
BF = jnp.bfloat16
F32 = jnp.float32


def holder(coil, quarter, low):
    z = (low // 4 * 2 - 2 + 4 * (coil % 2) + low % 2) % 8
    y = low % 4 // 2 * 2 + quarter % 2
    return (quarter // 2 * 32 + z * 4 + y) * 4 + coil


def reader(coil, group, low):
    return (group * 16 + low) * 4 + coil


def far_pairs(turn):
    return [
        (holder(c, q, low), reader((q // 2 ^ turn) * 2 + q % 2, c, low))
        for c in range(4)
        for q in range(4)
        for low in range(16)
    ]


def back_pairs(turn):
    return [(to, at) for at, to in far_pairs(turn)]


CORES = [(i, i ^ 1) for i in range(4)]
GROUPS = [[x * 32 + e + 2 * k for k in range(16)] for x in range(2) for e in range(2)]


def turned_by_core(data, coil, axis, sign):
    even = jnp.roll(data, sign, axis)
    odd = jnp.roll(data, -sign, axis)
    return jnp.where(coil % 2 == 0, even, odd)


def split(value):
    high = value.astype(BF)
    return high, (value - high.astype(F32)).astype(BF)


def split_outside(value):
    high = lax.reduce_precision(value, 8, 7)
    return high.astype(BF), (value - high).astype(BF)


def shifted(value, step):
    if step == 0:
        return value
    lane = lax.broadcasted_iota(jnp.int32, value.shape, value.ndim - 1)
    turned = pltpu.roll(value, step % 256, value.ndim - 1)
    edge = 0 if step > 0 else 255
    return jnp.where(lane == edge, 0.0, turned)


def filter_tables(weights):
    taps = np.zeros((3, 6, 8), np.float32)
    for d in range(3):
        for y in range(6):
            taps[d, y, y + d] = 1.0
    kernel = weights[0]
    ahead = sum(
        kernel[:, :, :, d][:, :, :, :, None, None] * taps[d] for d in range(3)
    )
    ahead = ahead.transpose(4, 0, 3, 2, 1, 5).reshape(288, 144)
    back = np.zeros((3, 4, 6), np.float32)
    for d in range(3):
        for y in range(4):
            back[d, y, y + 2 - d] = 1.0
    behind = sum(
        kernel[:, :, :, d][:, :, :, :, None, None] * back[d] for d in range(3)
    )
    behind = behind.transpose(2, 3, 1, 4, 5, 0).reshape(72, 288)
    high, low = split_outside(ahead)
    wide = jnp.concatenate([high, low, high], axis=1)
    high, low = split_outside(behind)
    turned = jnp.concatenate(
        [
            jnp.concatenate([high, high], axis=1),
            jnp.concatenate([low, jnp.zeros_like(low)], axis=1),
        ],
        axis=0,
    )
    return wide, turned


def window(packed, place, part):
    start = pl.multiple_of(place * 16, 16)
    return jnp.concatenate(
        [packed[d, part, pl.ds(start, 48)] for d in range(3)], axis=0
    )


def forward(place, table, packed):
    high = window(packed, place, 0)
    low = window(packed, place, 1)
    data = jnp.concatenate([high, high, low], axis=0)
    return jnp.dot(table, data, preferred_element_type=F32), high, low


def conv_kernel(
    init, grad, before, after, lower, upper, wide, xb, sums, xs, gs, gb
):
    gs[:, :, 0:1] = jnp.zeros((18, 2, 1, 256), F32)
    gs[:, :, 7:8] = jnp.zeros((18, 2, 1, 256), F32)
    for i in range(2):
        xs[2:18, i, 2:6] = init[i]
        for k in range(2):
            xs[2:18, i, k : k + 1] = before[2 * k + i].reshape(16, 1, 256)
            xs[2:18, i, k + 6 : k + 7] = after[2 * k + i].reshape(16, 1, 256)
        xs[0:2, i] = lower[2 * i : 2 * i + 2]
        xs[18:20, i] = upper[2 * i : 2 * i + 2]
        gs[1:17, i, 2:6] = grad[i]
        gs[1:17, i, 1:2] = before[4 + i].reshape(16, 1, 256)
        gs[1:17, i, 6:7] = after[4 + i].reshape(16, 1, 256)
        gs[0:1, i, 1:7] = lower[4 + i : 5 + i, 0:6]
        gs[17:18, i, 1:7] = upper[4 + i : 5 + i, 0:6]
    for plain, packed, count in ((xs, xb, 320), (gs, gb, 288)):
        value = plain[...].reshape(count, 256)
        for d in range(3):
            high, low = split(shifted(value, 1 - d))
            packed[d, 0] = high
            packed[d, 1] = low
    sums[...] = jnp.zeros_like(sums)

    def step(r, carry):
        response, xh, xl = forward(r + 1, wide[48:240], xb)
        linear, gh, gl = forward(r, wide[48:240], gb)
        core = jnp.tanh(response)
        weighted = (1.0 - core * core) * linear
        ch, cl = split(core)
        wh, wl = split(weighted)
        left = jnp.concatenate([gh, gh, gl, xh, xh, xl], axis=1)
        right = jnp.concatenate([ch, cl, ch, wh, wl, wh], axis=1)
        sums[...] += lax.dot_general(
            left, right, (((1,), (1,)), ((), ())), preferred_element_type=F32
        )
        return carry

    lax.fori_loop(0, 16, step, 0)


def adjoint_kernel(edge, init, xb, wide, turned, base, acc):
    acc[...] = jnp.zeros_like(acc)
    row = lax.broadcasted_iota(jnp.int32, (288, 256), 0)
    keep = jnp.where(row < 48, edge[0], jnp.where(row >= 240, edge[1], 1.0))

    def step(place, carry):
        scale = jnp.where(place == 0, edge[2], jnp.where(place == 17, edge[3], 1.0))
        response, _, _ = forward(place, wide[...], xb)
        high, low = split(jnp.tanh(response) * (keep * scale))
        data = jnp.concatenate([high, low], axis=0)
        product = jnp.dot(turned[...], data, preferred_element_type=F32)
        product = product[:72] + product[72:]
        for r in range(3):
            for d in range(3):
                first = (r * 3 + d) * 8
                acc[d, pl.ds(place + r, 1)] += product[first : first + 8][None]
        return carry

    lax.fori_loop(0, 18, step, 0)
    total = (
        shifted(acc[0, 2:18].reshape(128, 256), -1)
        + acc[1, 2:18].reshape(128, 256)
        + shifted(acc[2, 2:18].reshape(128, 256), 1)
    ).reshape(16, 8, 256)
    for i in range(2):
        base[i] = init[i] - total[:, 4 * i : 4 * i + 4]


VM = pl.BlockSpec(memory_space=pltpu.VMEM)
SM = pl.BlockSpec(memory_space=pltpu.SMEM)


def conv_call(init, grad, before, after, lower, upper, wide):
    return pl.pallas_call(
        conv_kernel,
        out_shape=(
            jax.ShapeDtypeStruct((3, 2, 320, 256), BF),
            jax.ShapeDtypeStruct((144, 192), F32),
        ),
        in_specs=[VM] * 7,
        out_specs=(VM, VM),
        scratch_shapes=[
            pltpu.VMEM((20, 2, 8, 256), F32),
            pltpu.VMEM((18, 2, 8, 256), F32),
            pltpu.VMEM((3, 2, 288, 256), BF),
        ],
        cost_estimate=pl.CostEstimate(
            flops=4000000000, bytes_accessed=2000000, transcendentals=800000
        ),
    )(init, grad, before, after, lower, upper, wide)


def adjoint_call(edge, init, xb, wide, turned):
    return pl.pallas_call(
        adjoint_kernel,
        out_shape=jax.ShapeDtypeStruct((2, 16, 4, 256), F32),
        in_specs=[SM] + [VM] * 4,
        out_specs=VM,
        scratch_shapes=[pltpu.VMEM((3, 20, 8, 256), F32)],
        cost_estimate=pl.CostEstimate(
            flops=4000000000, bytes_accessed=2000000, transcendentals=1300000
        ),
    )(edge, init, xb, wide, turned)


def diagonal(sums):
    cube = sums.reshape(3, 3, 2, 8, 4, 48)
    taps = [
        sum(cube[:, :, :, y + 1 + d, y] for y in range(4)) for d in range(3)
    ]
    return jnp.stack(taps, axis=3)


def tables():
    place = np.arange(256)
    mixed = (place // 128 * 32 + place // 64 % 2 + place % 16 * 2) * 4
    mixed = mixed + place // 16 % 4
    made = []
    for first, second in ((place, place), (place, mixed), (mixed, place)):
        angle = (first[:, None] * second[None, :] % 256) * (2.0 * np.pi / 256)
        for table in (np.cos(angle) / 16.0, np.sin(angle) / 16.0):
            table = np.asarray(table, np.float32)
            high = table.astype(BF)
            made.append(high)
            made.append((table - high.astype(np.float32)).astype(BF))
    return np.stack(made)


def transform_kernel(
    coil, maps, p0, p1, p2, p3, kspace, mask, extra, table, kept, sent, rows, right, left, lhs, rhs,
):
    here = coil[0]
    pieces = (p0, p1, p2, p3)

    def slot(a, q):
        return (q // 2 ^ a // 2) + 2 * (q % 2 ^ a % 2)

    for a in range(4):
        @pl.when(here == a)
        def _():
            for q in range(4):
                rows[q] = pieces[slot(a, q)][...]
    for part in range(2):
        cosine, sine = table[part], table[2 + part]
        right[part, :256, :256] = cosine
        right[part, :256, 256:] = -sine
        right[part, 256:, :256] = sine
        right[part, 256:, 256:] = cosine
    for part in range(4):
        first = 4 + part // 2 * 4 + part % 2
        cosine, sine = table[first], table[first + 2]
        left[part, :256, :256] = cosine
        left[part, :256, 256:] = sine
        left[part, 256:, :256] = -sine
        left[part, 256:, 256:] = cosine

    def halves(load):
        return jnp.concatenate(
            [
                jnp.concatenate([load(q, y, h) for h in range(2)], axis=1)
                for q in range(4)
                for y in range(4)
            ],
            axis=0,
        )

    def map_of(part, c):
        def load(q, y, h):
            first = (q // 2 * 32 + q % 2) * 32 + (y * 4 + part * 2 + c) * 2 + h
            return maps[pl.ds(first, 16, stride=64), :]

        return halves(load)

    def image_of(which, part):
        def load(q, y, h):
            return rows[q, pl.ds((which * 8 + part * 4 + y) * 2 + h, 16, stride=32), :]

        return halves(load)

    def transform(pairs, side):
        for c in range(2):
            for part in range(2):
                high, low = split(pairs[c][part])
                lhs[0, c * 256 : c * 256 + 256, part * 256 : part * 256 + 256] = high
                lhs[1, c * 256 : c * 256 + 256, part * 256 : part * 256 + 256] = low
        for c in range(2):
            block = slice(c * 256, c * 256 + 256)
            value = (
                jnp.dot(lhs[0, block], right[0], preferred_element_type=F32)
                + jnp.dot(lhs[1, block], right[0], preferred_element_type=F32)
                + jnp.dot(lhs[0, block], right[1], preferred_element_type=F32)
            )
            for part in range(2):
                high, low = split(value[:, part * 256 : part * 256 + 256])
                rhs[0, part * 256 : part * 256 + 256, block] = high
                rhs[1, part * 256 : part * 256 + 256, block] = low
        out = []
        for part in range(2):
            block = slice(part * 256, part * 256 + 256)
            out.append(
                jnp.dot(left[side, block], rhs[0], preferred_element_type=F32)
                + jnp.dot(left[side, block], rhs[1], preferred_element_type=F32)
                + jnp.dot(left[side + 1, block], rhs[0], preferred_element_type=F32)
            )
        return [
            [out[part][:, c * 256 : c * 256 + 256] for part in range(2)]
            for c in range(2)
        ]

    vr, vi = image_of(0, 0), image_of(0, 1)
    pairs = []
    for c in range(2):
        sr, si = map_of(0, c), map_of(1, c)
        pairs.append([sr * vr - si * vi, sr * vi + si * vr])
    pairs = transform(pairs, 0)
    keep = mask[...].astype(F32)

    pairs = [
        [
            (pairs[c][0] - kspace[0, c]) * keep,
            (kspace[1, c] - pairs[c][1]) * keep,
        ]
        for c in range(2)
    ]
    pairs = transform(pairs, 2)
    back_re = 0.0
    back_im = 0.0
    for c in range(2):
        sr, si = map_of(0, c), map_of(1, c)
        xr, xi = pairs[c][0], -pairs[c][1]
        back_re = back_re + sr * xr + si * xi
        back_im = back_im + sr * xi - si * xr
    back = (back_re, back_im)
    product = jnp.sum(
        back_re * image_of(1, 0) + back_im * image_of(1, 1), axis=0, keepdims=True
    )
    product = product[:, :128] + product[:, 128:]
    for out in (kept, sent):
        for t in range(2):
            out[t, 256:280] = extra[...]
            out[t, 278:279] = -product
    for a in range(4):
        @pl.when(here == a)
        def _():
            for q in range(4):
                place = slot(a, q)
                out = sent if place >= 2 else kept
                for part in range(2):
                    for y in range(4):
                        for h in range(2):
                            first = (part * 4 + y) * 2 + h
                            out[place % 2, pl.ds(first, 16, stride=16), :] = back[part][
                                q * 64 + y * 16 : q * 64 + y * 16 + 16,
                                h * 128 : h * 128 + 128,
                            ]


def transform_call(coil, maps, pieces, kspace, mask, extra):
    vm = pl.BlockSpec(memory_space=pltpu.VMEM)
    return pl.pallas_call(
        transform_kernel,
        out_shape=tuple(jax.ShapeDtypeStruct((2, 280, 128), F32) for _ in range(2)),
        in_specs=[pl.BlockSpec(memory_space=pltpu.SMEM)] + [vm] * 9,
        out_specs=(vm,) * 2,
        scratch_shapes=[
            pltpu.VMEM((4, 512, 128), F32),
            pltpu.VMEM((2, 512, 512), BF),
            pltpu.VMEM((4, 512, 512), BF),
            pltpu.VMEM((2, 512, 512), BF),
            pltpu.VMEM((2, 512, 512), BF),
        ],
        cost_estimate=pl.CostEstimate(
            flops=6000000000, bytes_accessed=5000000, transcendentals=0
        ),
    )(coil, maps, *pieces, kspace, mask, extra, jnp.asarray(tables()))


def halos(state, grad, slab_count):
    up = [(i, i + 1) for i in range(slab_count - 1)]
    down = [(i + 1, i) for i in range(slab_count - 1)]

    def pack(first, second, third):
        return jnp.concatenate(
            [state[:, :, first], state[:, :, second], grad[:, :, third]], axis=0
        )

    before = lax.ppermute(pack(2, 3, 3), "slab", up)
    after = lax.ppermute(pack(0, 1, 0), "slab", down)

    def planes(at, last):
        head = before[:4, at].reshape(2, 2, 2, 256).transpose(1, 2, 0, 3)
        tail = after[:4, at].reshape(2, 2, 2, 256).transpose(1, 2, 0, 3)
        rows = jnp.concatenate([head, state[:, at], tail], axis=2).reshape(4, 8, 256)
        edge = jnp.concatenate(
            [before[4:, last, None], grad[:, last], after[4:, last, None]], axis=1
        )
        return jnp.concatenate([rows, jnp.pad(edge, ((0, 0), (0, 2), (0, 0)))], axis=0)

    up = [(i, i + 1) for i in range(3)]
    down = [(i + 1, i) for i in range(3)]
    lower = lax.ppermute(planes(slice(14, 16), 15), "coil", up)
    upper = lax.ppermute(planes(slice(0, 2), 0), "coil", down)
    return before, after, lower, upper


def on_device(init_image, sens, kspace, mask, weights, step_sizes, recon_cotangent):
    slab_count = lax.axis_size("slab")
    coil = lax.axis_index("coil")
    slab = lax.axis_index("slab")
    images = jnp.stack([init_image, recon_cotangent]).reshape(2, 2, 4, 2, 2, 4, 256)
    images = images.transpose(2, 4, 3, 0, 1, 5, 6)
    images = turned_by_core(images, coil, 0, -1).reshape(16, 32, 128)
    images = lax.all_to_all(
        images, "slab", split_axis=0, concat_axis=0, tiled=True,
        axis_index_groups=GROUPS,
    )
    maps = sens.transpose(2, 3, 0, 1, 4).reshape(64, 32, 128)
    maps, images = lax.optimization_barrier((maps, images))
    received = lax.all_to_all(maps, "slab", split_axis=0, concat_axis=0, tiled=True)

    before, after, lower, upper = halos(init_image, recon_cotangent, slab_count)
    wide, turned = filter_tables(weights)
    edge = jnp.stack([slab > 0, slab < slab_count - 1, coil > 0, coil < 3]).astype(F32)
    packed, sums = conv_call(
        init_image, recon_cotangent, before, after, lower, upper, wide
    )
    extra = jnp.pad(-diagonal(sums).reshape(2592), (0, 480)).reshape(24, 128)

    held = images.reshape(512, 128)
    pieces = [lax.ppermute(held, AXES, far_pairs(turn)) for turn in range(2)]
    pieces = pieces + [lax.ppermute(piece, "coil", CORES) for piece in pieces]
    kept, sent = transform_call(
        coil.reshape(1), received.reshape(2048, 128), pieces, kspace[:, :, 0], mask,
        extra,
    )
    kept = kept + lax.ppermute(sent, "coil", CORES)
    total = lax.ppermute(kept[0], AXES, back_pairs(0)) + lax.ppermute(
        kept[1], AXES, back_pairs(1)
    )
    rider = jnp.broadcast_to(total[None, 256:], (16, 24, 128))
    sent = jnp.concatenate([total[:256].reshape(16, 16, 128), rider], axis=1)
    arrived = lax.all_to_all(
        sent, "slab", split_axis=0, concat_axis=0, tiled=True,
        axis_index_groups=GROUPS,
    )
    base = adjoint_call(edge, init_image, packed, wide, turned)
    own = jnp.sum(arrived[:, 16:], axis=0)
    riders = own
    for turn in range(1, 4):
        riders = riders + lax.ppermute(
            own, "coil", [(i, (i + turn) % 4) for i in range(4)]
        )
    combined = arrived[:, :16].reshape(4, 2, 2, 2, 4, 256)
    combined = turned_by_core(combined, coil, 0, 1).transpose(3, 0, 2, 1, 4, 5)
    recon = base - step_sizes[0] * combined.reshape(2, 16, 4, 256)
    step_grads = jnp.sum(riders[22])[None]
    grads = riders[:21].reshape(2688)[:2592]
    grads = grads.reshape(3, 3, 2, 3, 48).transpose(4, 2, 1, 3, 0)
    return recon, grads[None], step_grads


def solution(mesh):
    return jax.shard_map(
        on_device,
        mesh=mesh,
        in_specs=(
            P(None, "coil", "slab", None),
            P(None, "coil", None, "slab", None),
            P(None, "coil", "slab", None, None),
            P(),
            P(),
            P(),
            P(None, "coil", "slab", None),
        ),
        out_specs=(P(None, "coil", "slab", None), P(), P()),
        check_vma=False,
    )
```

```python
import jax
import jax.numpy as jnp
import numpy as np
from jax import lax
from jax.experimental import pallas as pl
from jax.experimental.pallas import tpu as pltpu
from jax.sharding import PartitionSpec as P

AXES = ("slab", "coil")
BF = jnp.bfloat16
F32 = jnp.float32


def holder(coil, quarter, low):
    z = (low // 4 - 1 + 2 * (coil % 2)) % 4 * 2 + quarter % 2
    return (quarter // 2 * 32 + z * 4 + low % 4) * 4 + coil


def reader(coil, group, low):
    return (group * 16 + low) * 4 + coil


def far_pairs(turn):
    return [
        (holder(c, q, low), reader((q // 2 ^ turn) * 2 + q % 2, c, low))
        for c in range(4)
        for q in range(4)
        for low in range(16)
    ]


def back_pairs(turn):
    return [(to, at) for at, to in far_pairs(turn)]


CORES = [(i, i ^ 1) for i in range(4)]


def turned_by_core(data, coil, axis, sign):
    even = jnp.roll(data, sign, axis)
    odd = jnp.roll(data, -sign, axis)
    return jnp.where(coil % 2 == 0, even, odd)


def split(value):
    high = value.astype(BF)
    return high, (value - high.astype(F32)).astype(BF)


def split_outside(value):
    high = lax.reduce_precision(value, 8, 7)
    return high.astype(BF), (value - high).astype(BF)


def shifted(value, step):
    if step == 0:
        return value
    lane = lax.broadcasted_iota(jnp.int32, value.shape, value.ndim - 1)
    turned = pltpu.roll(value, step % 256, value.ndim - 1)
    edge = 0 if step > 0 else 255
    return jnp.where(lane == edge, 0.0, turned)


def filter_tables(weights):
    taps = np.zeros((3, 6, 8), np.float32)
    for d in range(3):
        for y in range(6):
            taps[d, y, y + d] = 1.0
    kernel = weights[0]
    ahead = sum(
        kernel[:, :, :, d][:, :, :, :, None, None] * taps[d] for d in range(3)
    )
    ahead = ahead.transpose(4, 0, 3, 2, 1, 5).reshape(288, 144)
    back = np.zeros((3, 4, 6), np.float32)
    for d in range(3):
        for y in range(4):
            back[d, y, y + 2 - d] = 1.0
    behind = sum(
        kernel[:, :, :, d][:, :, :, :, None, None] * back[d] for d in range(3)
    )
    behind = behind.transpose(2, 3, 1, 4, 5, 0).reshape(72, 288)
    high, low = split_outside(ahead)
    wide = jnp.concatenate([high, low, high], axis=1)
    high, low = split_outside(behind)
    turned = jnp.concatenate(
        [
            jnp.concatenate([high, high], axis=1),
            jnp.concatenate([low, jnp.zeros_like(low)], axis=1),
        ],
        axis=0,
    )
    return wide, turned


def window(packed, place, part):
    start = pl.multiple_of(place * 16, 16)
    return jnp.concatenate(
        [packed[d, part, pl.ds(start, 48)] for d in range(3)], axis=0
    )


def forward(place, table, packed):
    high = window(packed, place, 0)
    low = window(packed, place, 1)
    data = jnp.concatenate([high, high, low], axis=0)
    return jnp.dot(table, data, preferred_element_type=F32), high, low


def conv_kernel(
    init, grad, before, after, lower, upper, wide, xb, sums, xs, gs, gb
):
    gs[:, :, 0:1] = jnp.zeros((18, 2, 1, 256), F32)
    gs[:, :, 7:8] = jnp.zeros((18, 2, 1, 256), F32)
    for i in range(2):
        xs[2:18, i, 2:6] = init[i]
        for k in range(2):
            xs[2:18, i, k : k + 1] = before[2 * k + i].reshape(16, 1, 256)
            xs[2:18, i, k + 6 : k + 7] = after[2 * k + i].reshape(16, 1, 256)
        xs[0:2, i] = lower[2 * i : 2 * i + 2]
        xs[18:20, i] = upper[2 * i : 2 * i + 2]
        gs[1:17, i, 2:6] = grad[i]
        gs[1:17, i, 1:2] = before[4 + i].reshape(16, 1, 256)
        gs[1:17, i, 6:7] = after[4 + i].reshape(16, 1, 256)
        gs[0:1, i, 1:7] = lower[4 + i : 5 + i, 0:6]
        gs[17:18, i, 1:7] = upper[4 + i : 5 + i, 0:6]
    for plain, packed, count in ((xs, xb, 320), (gs, gb, 288)):
        value = plain[...].reshape(count, 256)
        for d in range(3):
            high, low = split(shifted(value, 1 - d))
            packed[d, 0] = high
            packed[d, 1] = low
    sums[...] = jnp.zeros_like(sums)

    def step(r, carry):
        response, xh, xl = forward(r + 1, wide[48:240], xb)
        linear, gh, gl = forward(r, wide[48:240], gb)
        core = jnp.tanh(response)
        weighted = (1.0 - core * core) * linear
        ch, cl = split(core)
        wh, wl = split(weighted)
        left = jnp.concatenate([gh, gh, gl, xh, xh, xl], axis=1)
        right = jnp.concatenate([ch, cl, ch, wh, wl, wh], axis=1)
        sums[...] += lax.dot_general(
            left, right, (((1,), (1,)), ((), ())), preferred_element_type=F32
        )
        return carry

    lax.fori_loop(0, 16, step, 0)


def adjoint_kernel(edge, init, xb, wide, turned, base, acc):
    acc[...] = jnp.zeros_like(acc)
    row = lax.broadcasted_iota(jnp.int32, (288, 256), 0)
    keep = jnp.where(row < 48, edge[0], jnp.where(row >= 240, edge[1], 1.0))

    def step(place, carry):
        scale = jnp.where(place == 0, edge[2], jnp.where(place == 17, edge[3], 1.0))
        response, _, _ = forward(place, wide[...], xb)
        high, low = split(jnp.tanh(response) * (keep * scale))
        data = jnp.concatenate([high, low], axis=0)
        product = jnp.dot(turned[...], data, preferred_element_type=F32)
        product = product[:72] + product[72:]
        for r in range(3):
            for d in range(3):
                first = (r * 3 + d) * 8
                acc[d, pl.ds(place + r, 1)] += product[first : first + 8][None]
        return carry

    lax.fori_loop(0, 18, step, 0)
    total = (
        shifted(acc[0, 2:18].reshape(128, 256), -1)
        + acc[1, 2:18].reshape(128, 256)
        + shifted(acc[2, 2:18].reshape(128, 256), 1)
    ).reshape(16, 8, 256)
    for i in range(2):
        base[i] = init[i] - total[:, 4 * i : 4 * i + 4]


VM = pl.BlockSpec(memory_space=pltpu.VMEM)
SM = pl.BlockSpec(memory_space=pltpu.SMEM)


def conv_call(init, grad, before, after, lower, upper, wide):
    return pl.pallas_call(
        conv_kernel,
        out_shape=(
            jax.ShapeDtypeStruct((3, 2, 320, 256), BF),
            jax.ShapeDtypeStruct((144, 192), F32),
        ),
        in_specs=[VM] * 7,
        out_specs=(VM, VM),
        scratch_shapes=[
            pltpu.VMEM((20, 2, 8, 256), F32),
            pltpu.VMEM((18, 2, 8, 256), F32),
            pltpu.VMEM((3, 2, 288, 256), BF),
        ],
        cost_estimate=pl.CostEstimate(
            flops=4000000000, bytes_accessed=2000000, transcendentals=800000
        ),
    )(init, grad, before, after, lower, upper, wide)


def adjoint_call(edge, init, xb, wide, turned):
    return pl.pallas_call(
        adjoint_kernel,
        out_shape=jax.ShapeDtypeStruct((2, 16, 4, 256), F32),
        in_specs=[SM] + [VM] * 4,
        out_specs=VM,
        scratch_shapes=[pltpu.VMEM((3, 20, 8, 256), F32)],
        cost_estimate=pl.CostEstimate(
            flops=4000000000, bytes_accessed=2000000, transcendentals=1300000
        ),
    )(edge, init, xb, wide, turned)


def diagonal(sums):
    cube = sums.reshape(3, 3, 2, 8, 4, 48)
    taps = [
        sum(cube[:, :, :, y + 1 + d, y] for y in range(4)) for d in range(3)
    ]
    return jnp.stack(taps, axis=3)


def tables():
    place = np.arange(256)
    mixed = place % 64 * 4 + place // 64
    made = []
    for first, second in ((place, place), (place, mixed), (mixed, place)):
        angle = (first[:, None] * second[None, :] % 256) * (2.0 * np.pi / 256)
        for table in (np.cos(angle) / 16.0, np.sin(angle) / 16.0):
            table = np.asarray(table, np.float32)
            high = table.astype(BF)
            made.append(high)
            made.append((table - high.astype(np.float32)).astype(BF))
    return np.stack(made)


def transform_kernel(
    coil, maps, p0, p1, p2, p3, kspace, mask, extra, table, kept, sent, rows, right, left, lhs, rhs,
):
    here = coil[0]
    pieces = (p0, p1, p2, p3)

    def slot(a, q):
        return (q // 2 ^ a // 2) + 2 * (q % 2 ^ a % 2)

    for a in range(4):
        @pl.when(here == a)
        def _():
            for q in range(4):
                rows[q] = pieces[slot(a, q)][...]
    for part in range(2):
        cosine, sine = table[part], table[2 + part]
        right[part, :256, :256] = cosine
        right[part, :256, 256:] = -sine
        right[part, 256:, :256] = sine
        right[part, 256:, 256:] = cosine
    for part in range(4):
        first = 4 + part // 2 * 4 + part % 2
        cosine, sine = table[first], table[first + 2]
        left[part, :256, :256] = cosine
        left[part, :256, 256:] = sine
        left[part, 256:, :256] = -sine
        left[part, 256:, 256:] = cosine

    def halves(load):
        return jnp.concatenate(
            [
                jnp.concatenate([load(y, h) for h in range(2)], axis=1)
                for y in range(4)
            ],
            axis=0,
        )

    def map_of(part, c):
        return halves(
            lambda y, h: maps[pl.ds((y * 4 + part * 2 + c) * 2 + h, 64, stride=40), :]
        )

    def image_of(part):
        return halves(lambda y, h: rows[y, pl.ds(part * 2 + h, 64, stride=4), :])

    def transform(pairs, side):
        for c in range(2):
            for part in range(2):
                high, low = split(pairs[c][part])
                lhs[0, c * 256 : c * 256 + 256, part * 256 : part * 256 + 256] = high
                lhs[1, c * 256 : c * 256 + 256, part * 256 : part * 256 + 256] = low
        for c in range(2):
            block = slice(c * 256, c * 256 + 256)
            value = (
                jnp.dot(lhs[0, block], right[0], preferred_element_type=F32)
                + jnp.dot(lhs[1, block], right[0], preferred_element_type=F32)
                + jnp.dot(lhs[0, block], right[1], preferred_element_type=F32)
            )
            for part in range(2):
                high, low = split(value[:, part * 256 : part * 256 + 256])
                rhs[0, part * 256 : part * 256 + 256, block] = high
                rhs[1, part * 256 : part * 256 + 256, block] = low
        out = []
        for part in range(2):
            block = slice(part * 256, part * 256 + 256)
            out.append(
                jnp.dot(left[side, block], rhs[0], preferred_element_type=F32)
                + jnp.dot(left[side, block], rhs[1], preferred_element_type=F32)
                + jnp.dot(left[side + 1, block], rhs[0], preferred_element_type=F32)
            )
        return [
            [out[part][:, c * 256 : c * 256 + 256] for part in range(2)]
            for c in range(2)
        ]

    vr, vi = image_of(0), image_of(1)
    pairs = []
    for c in range(2):
        sr, si = map_of(0, c), map_of(1, c)
        pairs.append([sr * vr - si * vi, sr * vi + si * vr])
    pairs = transform(pairs, 0)
    keep = mask[...].astype(F32)

    pairs = [
        [
            (pairs[c][0] - kspace[0, c]) * keep,
            (kspace[1, c] - pairs[c][1]) * keep,
        ]
        for c in range(2)
    ]
    pairs = transform(pairs, 2)
    back_re = 0.0
    back_im = 0.0
    for c in range(2):
        sr, si = map_of(0, c), map_of(1, c)
        xr, xi = pairs[c][0], -pairs[c][1]
        back_re = back_re + sr * xr + si * xi
        back_im = back_im + sr * xi - si * xr
    back = (back_re, back_im)
    for out in (kept, sent):
        for t in range(2):
            out[t, 256:280] = extra[...]
    for a in range(4):
        @pl.when(here == a)
        def _():
            for q in range(4):
                place = slot(a, q)
                out = sent if place >= 2 else kept
                for part in range(2):
                    for h in range(2):
                        out[place % 2, pl.ds(part * 2 + h, 64, stride=4), :] = back[
                            part
                        ][q * 64 : q * 64 + 64, h * 128 : h * 128 + 128]


def transform_call(coil, maps, pieces, kspace, mask, extra):
    vm = pl.BlockSpec(memory_space=pltpu.VMEM)
    return pl.pallas_call(
        transform_kernel,
        out_shape=tuple(jax.ShapeDtypeStruct((2, 280, 128), F32) for _ in range(2)),
        in_specs=[pl.BlockSpec(memory_space=pltpu.SMEM)] + [vm] * 9,
        out_specs=(vm,) * 2,
        scratch_shapes=[
            pltpu.VMEM((4, 256, 128), F32),
            pltpu.VMEM((2, 512, 512), BF),
            pltpu.VMEM((4, 512, 512), BF),
            pltpu.VMEM((2, 512, 512), BF),
            pltpu.VMEM((2, 512, 512), BF),
        ],
        cost_estimate=pl.CostEstimate(
            flops=6000000000, bytes_accessed=5000000, transcendentals=0
        ),
    )(coil, maps, *pieces, kspace, mask, extra, jnp.asarray(tables()))


def halos(state, grad, slab_count):
    up = [(i, i + 1) for i in range(slab_count - 1)]
    down = [(i + 1, i) for i in range(slab_count - 1)]

    def pack(first, second, third):
        return jnp.concatenate(
            [state[:, :, first], state[:, :, second], grad[:, :, third]], axis=0
        )

    before = lax.ppermute(pack(2, 3, 3), "slab", up)
    after = lax.ppermute(pack(0, 1, 0), "slab", down)

    def planes(at, last):
        head = before[:4, at].reshape(2, 2, 2, 256).transpose(1, 2, 0, 3)
        tail = after[:4, at].reshape(2, 2, 2, 256).transpose(1, 2, 0, 3)
        rows = jnp.concatenate([head, state[:, at], tail], axis=2).reshape(4, 8, 256)
        edge = jnp.concatenate(
            [before[4:, last, None], grad[:, last], after[4:, last, None]], axis=1
        )
        return jnp.concatenate([rows, jnp.pad(edge, ((0, 0), (0, 2), (0, 0)))], axis=0)

    up = [(i, i + 1) for i in range(3)]
    down = [(i + 1, i) for i in range(3)]
    lower = lax.ppermute(planes(slice(14, 16), 15), "coil", up)
    upper = lax.ppermute(planes(slice(0, 2), 0), "coil", down)
    return before, after, lower, upper


def on_device(init_image, sens, kspace, mask, weights, step_sizes, recon_cotangent):
    slab_count = lax.axis_size("slab")
    coil = lax.axis_index("coil")
    slab = lax.axis_index("slab")
    maps = sens.transpose(2, 3, 0, 1, 4).reshape(64, 16, 2, 128)
    images = jnp.stack([init_image, recon_cotangent]).reshape(2, 2, 4, 4, 2, 2, 256)
    images = images.transpose(4, 2, 5, 3, 0, 1, 6)
    images = turned_by_core(images, coil, 1, -1).reshape(64, 4, 2, 128)
    payload = jnp.concatenate([maps, images], axis=1)
    received = lax.all_to_all(payload, "slab", split_axis=0, concat_axis=0, tiled=True)

    before, after, lower, upper = halos(init_image, recon_cotangent, slab_count)
    wide, turned = filter_tables(weights)
    edge = jnp.stack([slab > 0, slab < slab_count - 1, coil > 0, coil < 3]).astype(F32)
    packed, sums = conv_call(
        init_image, recon_cotangent, before, after, lower, upper, wide
    )
    extra = jnp.pad(-diagonal(sums).reshape(4, 648), ((0, 0), (0, 120)))
    extra = extra.reshape(24, 128)

    held = received[:, 16:18].reshape(256, 128)
    pieces = [lax.ppermute(held, AXES, far_pairs(turn)) for turn in range(2)]
    pieces = pieces + [lax.ppermute(piece, "coil", CORES) for piece in pieces]
    kept, sent = transform_call(
        coil.reshape(1), received.reshape(2560, 128), pieces, kspace[:, :, 0], mask,
        extra,
    )
    kept = kept + lax.ppermute(sent, "coil", CORES)
    total = lax.ppermute(kept[0], AXES, back_pairs(0)) + lax.ppermute(
        kept[1], AXES, back_pairs(1)
    )
    product = jnp.sum(total[:256] * received[:, 18:20].reshape(256, 128))
    quarter = slab // 32 * 2 + slab // 4 % 2
    rider = lax.dynamic_slice_in_dim(total, 256 + 6 * quarter, 6, axis=0)
    corner = np.zeros((6, 128), np.float32)
    corner[5, 127] = 1.0
    rider = rider - product * corner
    rider = jnp.broadcast_to(rider.reshape(1, 3, 2, 128), (64, 3, 2, 128))
    sent = jnp.concatenate([total[:256].reshape(64, 2, 2, 128), rider], axis=1)
    arrived = lax.all_to_all(sent, "slab", split_axis=0, concat_axis=0, tiled=True)
    base = adjoint_call(edge, init_image, packed, wide, turned)
    own = jnp.sum(arrived[:, 2:].reshape(2, 4, 2, 4, 6, 128), axis=(1, 3))
    own = own.reshape(24, 128)
    riders = own
    for turn in range(1, 4):
        riders = riders + lax.ppermute(
            own, "coil", [(i, (i + turn) % 4) for i in range(4)]
        )
    combined = arrived[:, :2].reshape(2, 4, 2, 4, 2, 256)
    combined = turned_by_core(combined, coil, 1, 1).transpose(4, 1, 3, 0, 2, 5)
    recon = base - step_sizes[0] * combined.reshape(2, 16, 4, 256)
    riders = riders.reshape(4, 768)
    step_grads = jnp.sum(riders[:, 767])[None]
    grads = riders[:, :648].reshape(2592)
    grads = grads.reshape(3, 3, 2, 3, 48).transpose(4, 2, 1, 3, 0)
    return recon, grads[None], step_grads


def solution(mesh):
    return jax.shard_map(
        on_device,
        mesh=mesh,
        in_specs=(
            P(None, "coil", "slab", None),
            P(None, "coil", None, "slab", None),
            P(None, "coil", "slab", None, None),
            P(),
            P(),
            P(),
            P(None, "coil", "slab", None),
        ),
        out_specs=(P(None, "coil", "slab", None), P(), P()),
        check_vma=False,
    )
```

```python
import jax
import jax.numpy as jnp
import numpy as np
from jax import lax
from jax.experimental import pallas as pl
from jax.experimental.pallas import tpu as pltpu
from jax.sharding import PartitionSpec as P

AXES = ("slab", "coil")
BF = jnp.bfloat16
F32 = jnp.float32


def holder(coil, quarter, low):
    z = (low // 4 - 1 + 2 * (coil % 2)) % 4 * 2 + quarter % 2
    return (quarter // 2 * 32 + z * 4 + low % 4) * 4 + coil


def reader(coil, group, low):
    return (group * 16 + low) * 4 + coil


def far_pairs(turn):
    return [
        (holder(c, q, low), reader((q // 2 ^ turn) * 2 + q % 2, c, low))
        for c in range(4)
        for q in range(4)
        for low in range(16)
    ]


def back_pairs(turn):
    return [(to, at) for at, to in far_pairs(turn)]


CORES = [(i, i ^ 1) for i in range(4)]


VM = pl.BlockSpec(memory_space=pltpu.VMEM)
SM = pl.BlockSpec(memory_space=pltpu.SMEM)


def edge_kernel(odd, state, grad, near, next_pair):
    for parity in range(2):
        high, low = (near, next_pair) if parity == 0 else (next_pair, near)

        @pl.when(odd[0] == parity)
        def _():
            for i in range(2):
                for k in range(2):
                    high[2 * k + i] = state[i, :, 2 + k, :]
                    low[2 * k + i] = state[i, :, k, :]
                high[4 + i] = grad[i, :, 3, :]
                low[4 + i] = grad[i, :, 0, :]


def edge_call(odd, state, grad):
    shape = jax.ShapeDtypeStruct((6, 16, 256), F32)
    return pl.pallas_call(
        edge_kernel,
        out_shape=(shape, shape),
        in_specs=[SM, VM, VM],
        out_specs=(VM, VM),
        cost_estimate=pl.CostEstimate(
            flops=0, bytes_accessed=460000, transcendentals=0
        ),
    )(odd, state, grad)


def payload_kernel(coil, state, grad, maps, out):
    core = coil[0] % 2
    for part in range(2):
        for c in range(2):
            for r in range(64):
                for h in range(2):
                    first = r * 40 + (part * 2 + c) * 2 + h
                    out[pl.ds(first, 4, stride=8), :] = maps[
                        part, c, r, :, h * 128 : h * 128 + 128
                    ]
    for kind in range(2):
        for core_here in range(2):
            @pl.when(core == core_here)
            def _():
                field = (state, grad)[kind]
                for part in range(2):
                    for low in range(16):
                        z = (low // 4 - 1 + 2 * core_here) % 4
                        for h in range(2):
                            first = (z * 8 + low % 4) * 40 + (16 + kind * 2 + part) * 2 + h
                            rows = field[part, low, :, h * 128 : h * 128 + 128]
                            out[pl.ds(first, 2, stride=160), :] = rows[:2]
                            out[pl.ds(first + 1280, 2, stride=160), :] = rows[2:]


def payload_call(coil, state, grad, maps):
    return pl.pallas_call(
        payload_kernel,
        out_shape=jax.ShapeDtypeStruct((2560, 128), F32),
        in_specs=[SM, VM, VM, VM],
        out_specs=VM,
        cost_estimate=pl.CostEstimate(
            flops=0, bytes_accessed=2600000, transcendentals=0
        ),
    )(coil, state, grad, maps)


def combine_kernel(quarter, one, two, grad, out):
    product = 0.0
    for k in range(4):
        rows = pl.ds(k, 64, stride=4)
        total = one[rows, :] + two[rows, :]
        out[pl.ds(k, 64, stride=10), :] = total
        product = product + total * grad[rows, :]
    product = jnp.sum(product)
    first = 256 + 6 * quarter[0]
    lane = lax.broadcasted_iota(jnp.int32, (1, 128), 1)
    for k in range(6):
        rider = one[pl.ds(first + k, 1), :] + two[pl.ds(first + k, 1), :]
        if k == 5:
            rider = jnp.where(lane == 127, -product, rider)
        out[pl.ds(4 + k, 64, stride=10), :] = jnp.broadcast_to(rider, (64, 128))


def combine_call(quarter, one, two, grad):
    return pl.pallas_call(
        combine_kernel,
        out_shape=jax.ShapeDtypeStruct((640, 128), F32),
        in_specs=[SM, VM, VM, VM],
        out_specs=VM,
        cost_estimate=pl.CostEstimate(
            flops=100000, bytes_accessed=800000, transcendentals=0
        ),
    )(quarter, one, two, grad)


def turned_by_core(data, coil, axis, sign):
    even = jnp.roll(data, sign, axis)
    odd = jnp.roll(data, -sign, axis)
    return jnp.where(coil % 2 == 0, even, odd)


def split(value):
    high = value.astype(BF)
    return high, (value - high.astype(F32)).astype(BF)


def split_outside(value):
    high = lax.reduce_precision(value, 8, 7)
    return high.astype(BF), (value - high).astype(BF)


def shifted(value, step):
    if step == 0:
        return value
    lane = lax.broadcasted_iota(jnp.int32, value.shape, value.ndim - 1)
    turned = pltpu.roll(value, step % 256, value.ndim - 1)
    edge = 0 if step > 0 else 255
    return jnp.where(lane == edge, 0.0, turned)


def filter_tables(weights):
    taps = np.zeros((3, 6, 8), np.float32)
    for d in range(3):
        for y in range(6):
            taps[d, y, y + d] = 1.0
    kernel = weights[0]
    ahead = sum(
        kernel[:, :, :, d][:, :, :, :, None, None] * taps[d] for d in range(3)
    )
    ahead = ahead.transpose(4, 0, 3, 2, 1, 5).reshape(288, 144)
    back = np.zeros((3, 4, 6), np.float32)
    for d in range(3):
        for y in range(4):
            back[d, y, y + 2 - d] = 1.0
    behind = sum(
        kernel[:, :, :, d][:, :, :, :, None, None] * back[d] for d in range(3)
    )
    behind = behind.transpose(2, 3, 1, 4, 5, 0).reshape(72, 288)
    high, low = split_outside(ahead)
    wide = jnp.concatenate([high, low, high], axis=1)
    high, low = split_outside(behind)
    turned = jnp.concatenate(
        [
            jnp.concatenate([high, high], axis=1),
            jnp.concatenate([low, jnp.zeros_like(low)], axis=1),
        ],
        axis=0,
    )
    return wide, turned


def window(packed, place, part):
    start = pl.multiple_of(place * 16, 16)
    return jnp.concatenate(
        [packed[d, part, pl.ds(start, 48)] for d in range(3)], axis=0
    )


def forward(place, table, packed):
    high = window(packed, place, 0)
    low = window(packed, place, 1)
    data = jnp.concatenate([high, high, low], axis=0)
    return jnp.dot(table, data, preferred_element_type=F32), high, low


def conv_kernel(
    init, grad, before, after, lower, upper, wide, xb, sums, xs, gs, gb
):
    gs[:, :, 0:1] = jnp.zeros((18, 2, 1, 256), F32)
    gs[:, :, 7:8] = jnp.zeros((18, 2, 1, 256), F32)
    for i in range(2):
        xs[2:18, i, 2:6] = init[i]
        for k in range(2):
            xs[2:18, i, k : k + 1] = before[2 * k + i].reshape(16, 1, 256)
            xs[2:18, i, k + 6 : k + 7] = after[2 * k + i].reshape(16, 1, 256)
        xs[0:2, i] = lower[2 * i : 2 * i + 2]
        xs[18:20, i] = upper[2 * i : 2 * i + 2]
        gs[1:17, i, 2:6] = grad[i]
        gs[1:17, i, 1:2] = before[4 + i].reshape(16, 1, 256)
        gs[1:17, i, 6:7] = after[4 + i].reshape(16, 1, 256)
        gs[0:1, i, 1:7] = lower[4 + i : 5 + i, 0:6]
        gs[17:18, i, 1:7] = upper[4 + i : 5 + i, 0:6]
    for plain, packed, count in ((xs, xb, 320), (gs, gb, 288)):
        value = plain[...].reshape(count, 256)
        for d in range(3):
            high, low = split(shifted(value, 1 - d))
            packed[d, 0] = high
            packed[d, 1] = low
    sums[...] = jnp.zeros_like(sums)

    def step(r, carry):
        response, xh, xl = forward(r + 1, wide[48:240], xb)
        linear, gh, gl = forward(r, wide[48:240], gb)
        core = jnp.tanh(response)
        weighted = (1.0 - core * core) * linear
        ch, cl = split(core)
        wh, wl = split(weighted)
        left = jnp.concatenate([gh, gh, gl, xh, xh, xl], axis=1)
        right = jnp.concatenate([ch, cl, ch, wh, wl, wh], axis=1)
        sums[...] += lax.dot_general(
            left, right, (((1,), (1,)), ((), ())), preferred_element_type=F32
        )
        return carry

    lax.fori_loop(0, 16, step, 0)


def adjoint_kernel(edge, init, xb, wide, turned, base, acc):
    acc[...] = jnp.zeros_like(acc)
    row = lax.broadcasted_iota(jnp.int32, (288, 256), 0)
    keep = jnp.where(row < 48, edge[0], jnp.where(row >= 240, edge[1], 1.0))

    def step(place, carry):
        scale = jnp.where(place == 0, edge[2], jnp.where(place == 17, edge[3], 1.0))
        response, _, _ = forward(place, wide[...], xb)
        high, low = split(jnp.tanh(response) * (keep * scale))
        data = jnp.concatenate([high, low], axis=0)
        product = jnp.dot(turned[...], data, preferred_element_type=F32)
        product = product[:72] + product[72:]
        for r in range(3):
            for d in range(3):
                first = (r * 3 + d) * 8
                acc[d, pl.ds(place + r, 1)] += product[first : first + 8][None]
        return carry

    lax.fori_loop(0, 18, step, 0)
    total = (
        shifted(acc[0, 2:18].reshape(128, 256), -1)
        + acc[1, 2:18].reshape(128, 256)
        + shifted(acc[2, 2:18].reshape(128, 256), 1)
    ).reshape(16, 8, 256)
    for i in range(2):
        base[i] = init[i] - total[:, 4 * i : 4 * i + 4]


def conv_call(init, grad, before, after, lower, upper, wide):
    return pl.pallas_call(
        conv_kernel,
        out_shape=(
            jax.ShapeDtypeStruct((3, 2, 320, 256), BF),
            jax.ShapeDtypeStruct((144, 192), F32),
        ),
        in_specs=[VM] * 7,
        out_specs=(VM, VM),
        scratch_shapes=[
            pltpu.VMEM((20, 2, 8, 256), F32),
            pltpu.VMEM((18, 2, 8, 256), F32),
            pltpu.VMEM((3, 2, 288, 256), BF),
        ],
        cost_estimate=pl.CostEstimate(
            flops=4000000000, bytes_accessed=2000000, transcendentals=800000
        ),
    )(init, grad, before, after, lower, upper, wide)


def adjoint_call(edge, init, xb, wide, turned):
    return pl.pallas_call(
        adjoint_kernel,
        out_shape=jax.ShapeDtypeStruct((2, 16, 4, 256), F32),
        in_specs=[SM] + [VM] * 4,
        out_specs=VM,
        scratch_shapes=[pltpu.VMEM((3, 20, 8, 256), F32)],
        cost_estimate=pl.CostEstimate(
            flops=4000000000, bytes_accessed=2000000, transcendentals=1300000
        ),
    )(edge, init, xb, wide, turned)


def diagonal(sums):
    cube = sums.reshape(3, 3, 2, 8, 4, 48)
    taps = [
        sum(cube[:, :, :, y + 1 + d, y] for y in range(4)) for d in range(3)
    ]
    return jnp.stack(taps, axis=3)


def tables():
    place = np.arange(256)
    mixed = place % 64 * 4 + place // 64
    made = []
    for first, second in ((place, place), (place, mixed), (mixed, place)):
        angle = (first[:, None] * second[None, :] % 256) * (2.0 * np.pi / 256)
        for table in (np.cos(angle) / 16.0, np.sin(angle) / 16.0):
            table = np.asarray(table, np.float32)
            high = table.astype(BF)
            made.append(high)
            made.append((table - high.astype(np.float32)).astype(BF))
    return np.stack(made)


def transform_kernel(
    coil, maps, p0, p1, p2, p3, kspace, mask, extra, table, kept, sent, rows, right, left, lhs, rhs,
):
    here = coil[0]
    pieces = (p0, p1, p2, p3)

    def slot(a, q):
        return (q // 2 ^ a // 2) + 2 * (q % 2 ^ a % 2)

    for a in range(4):
        @pl.when(here == a)
        def _():
            for q in range(4):
                rows[q] = pieces[slot(a, q)][...]
    for part in range(2):
        cosine, sine = table[part], table[2 + part]
        right[part, :256, :256] = cosine
        right[part, :256, 256:] = -sine
        right[part, 256:, :256] = sine
        right[part, 256:, 256:] = cosine
    for part in range(4):
        first = 4 + part // 2 * 4 + part % 2
        cosine, sine = table[first], table[first + 2]
        left[part, :256, :256] = cosine
        left[part, :256, 256:] = sine
        left[part, 256:, :256] = -sine
        left[part, 256:, 256:] = cosine

    def halves(load):
        return jnp.concatenate(
            [
                jnp.concatenate([load(y, h) for h in range(2)], axis=1)
                for y in range(4)
            ],
            axis=0,
        )

    def map_of(part, c):
        return halves(
            lambda y, h: maps[pl.ds((y * 4 + part * 2 + c) * 2 + h, 64, stride=40), :]
        )

    def image_of(part):
        return halves(lambda y, h: rows[y, pl.ds(part * 2 + h, 64, stride=4), :])

    def transform(pairs, side):
        for c in range(2):
            for part in range(2):
                high, low = split(pairs[c][part])
                lhs[0, c * 256 : c * 256 + 256, part * 256 : part * 256 + 256] = high
                lhs[1, c * 256 : c * 256 + 256, part * 256 : part * 256 + 256] = low
        for c in range(2):
            block = slice(c * 256, c * 256 + 256)
            value = (
                jnp.dot(lhs[0, block], right[0], preferred_element_type=F32)
                + jnp.dot(lhs[1, block], right[0], preferred_element_type=F32)
                + jnp.dot(lhs[0, block], right[1], preferred_element_type=F32)
            )
            for part in range(2):
                high, low = split(value[:, part * 256 : part * 256 + 256])
                rhs[0, part * 256 : part * 256 + 256, block] = high
                rhs[1, part * 256 : part * 256 + 256, block] = low
        out = []
        for part in range(2):
            block = slice(part * 256, part * 256 + 256)
            out.append(
                jnp.dot(left[side, block], rhs[0], preferred_element_type=F32)
                + jnp.dot(left[side, block], rhs[1], preferred_element_type=F32)
                + jnp.dot(left[side + 1, block], rhs[0], preferred_element_type=F32)
            )
        return [
            [out[part][:, c * 256 : c * 256 + 256] for part in range(2)]
            for c in range(2)
        ]

    vr, vi = image_of(0), image_of(1)
    pairs = []
    for c in range(2):
        sr, si = map_of(0, c), map_of(1, c)
        pairs.append([sr * vr - si * vi, sr * vi + si * vr])
    pairs = transform(pairs, 0)
    keep = mask[...].astype(F32)

    pairs = [
        [
            (pairs[c][0] - kspace[0, c]) * keep,
            (kspace[1, c] - pairs[c][1]) * keep,
        ]
        for c in range(2)
    ]
    pairs = transform(pairs, 2)
    back_re = 0.0
    back_im = 0.0
    for c in range(2):
        sr, si = map_of(0, c), map_of(1, c)
        xr, xi = pairs[c][0], -pairs[c][1]
        back_re = back_re + sr * xr + si * xi
        back_im = back_im + sr * xi - si * xr
    back = (back_re, back_im)
    for out in (kept, sent):
        for t in range(2):
            out[t, 256:280] = extra[...]
    for a in range(4):
        @pl.when(here == a)
        def _():
            for q in range(4):
                place = slot(a, q)
                out = sent if place >= 2 else kept
                for part in range(2):
                    for h in range(2):
                        out[place % 2, pl.ds(part * 2 + h, 64, stride=4), :] = back[
                            part
                        ][q * 64 : q * 64 + 64, h * 128 : h * 128 + 128]


def transform_call(coil, maps, pieces, kspace, mask, extra):
    vm = pl.BlockSpec(memory_space=pltpu.VMEM)
    return pl.pallas_call(
        transform_kernel,
        out_shape=tuple(jax.ShapeDtypeStruct((2, 280, 128), F32) for _ in range(2)),
        in_specs=[pl.BlockSpec(memory_space=pltpu.SMEM)] + [vm] * 9,
        out_specs=(vm,) * 2,
        scratch_shapes=[
            pltpu.VMEM((4, 256, 128), F32),
            pltpu.VMEM((2, 512, 512), BF),
            pltpu.VMEM((4, 512, 512), BF),
            pltpu.VMEM((2, 512, 512), BF),
            pltpu.VMEM((2, 512, 512), BF),
        ],
        compiler_params=pltpu.CompilerParams(vmem_limit_bytes=32 << 20),
        cost_estimate=pl.CostEstimate(
            flops=6000000000, bytes_accessed=5000000, transcendentals=0
        ),
    )(coil, maps, *pieces, kspace, mask, extra, jnp.asarray(tables()))


def swapped(first, second):
    return [(first, second), (second, first)]


def halos(state, grad, slab_count):
    odd = lax.axis_index("slab") % 2
    pairs = [p for i in range(0, slab_count, 2) for p in swapped(i, i + 1)]
    others = [p for i in range(1, slab_count - 1, 2) for p in swapped(i, i + 1)]
    near, far = edge_call(odd.reshape(1), state, grad)
    near = lax.ppermute(near, "slab", pairs)
    far = lax.ppermute(far, "slab", others)
    before = jnp.where(odd == 0, far, near)
    after = jnp.where(odd == 0, near, far)

    def planes(at, last):
        head = before[:4, at].reshape(2, 2, 2, 256).transpose(1, 2, 0, 3)
        tail = after[:4, at].reshape(2, 2, 2, 256).transpose(1, 2, 0, 3)
        rows = jnp.concatenate([head, state[:, at], tail], axis=2).reshape(4, 8, 256)
        edge = jnp.concatenate(
            [before[4:, last, None], grad[:, last], after[4:, last, None]], axis=1
        )
        return jnp.concatenate([rows, jnp.pad(edge, ((0, 0), (0, 2), (0, 0)))], axis=0)

    odd = lax.axis_index("coil") % 2
    high, low = planes(slice(14, 16), 15), planes(slice(0, 2), 0)
    near = lax.ppermute(jnp.where(odd == 0, high, low), "coil", CORES)
    far = lax.ppermute(jnp.where(odd == 0, low, high), "coil", swapped(1, 2))
    lower = jnp.where(odd == 0, far, near)
    upper = jnp.where(odd == 0, near, far)
    return before, after, lower, upper


def on_device(init_image, sens, kspace, mask, weights, step_sizes, recon_cotangent):
    slab_count = lax.axis_size("slab")
    coil = lax.axis_index("coil")
    slab = lax.axis_index("slab")
    payload = payload_call(coil.reshape(1), init_image, recon_cotangent, sens)
    payload = payload.reshape(64, 20, 2, 128)
    received = lax.all_to_all(payload, "slab", split_axis=0, concat_axis=0, tiled=True)

    before, after, lower, upper = halos(init_image, recon_cotangent, slab_count)
    wide, turned = filter_tables(weights)
    edge = jnp.stack([slab > 0, slab < slab_count - 1, coil > 0, coil < 3]).astype(F32)
    lower, wide, turned, edge = lax.optimization_barrier((lower, wide, turned, edge))
    packed, sums = conv_call(
        init_image, recon_cotangent, before, after, lower, upper, wide
    )
    extra = jnp.pad(-diagonal(sums).reshape(4, 648), ((0, 0), (0, 120)))
    extra = extra.reshape(24, 128)

    held = received[:, 16:18].reshape(256, 128)
    pieces = [lax.ppermute(held, AXES, far_pairs(turn)) for turn in range(2)]
    pieces = pieces + [lax.ppermute(piece, "coil", CORES) for piece in pieces]
    kept, sent = transform_call(
        coil.reshape(1), received.reshape(2560, 128), pieces, kspace[:, :, 0], mask,
        extra,
    )
    kept = kept + lax.ppermute(sent, "coil", CORES)
    parts = [lax.ppermute(kept[t], AXES, back_pairs(t)) for t in range(2)]
    quarter = slab // 32 * 2 + slab // 4 % 2
    sent = combine_call(
        quarter.reshape(1), *parts, received[:, 18:20].reshape(256, 128)
    )
    sent = sent.reshape(64, 5, 2, 128)
    arrived = lax.all_to_all(sent, "slab", split_axis=0, concat_axis=0, tiled=True)
    base = adjoint_call(edge, init_image, packed, wide, turned)
    own = jnp.sum(arrived[:, 2:].reshape(2, 4, 2, 4, 6, 128), axis=(1, 3))
    own = own.reshape(24, 128)
    riders = own
    for turn in range(1, 4):
        riders = riders + lax.ppermute(
            own, "coil", [(i, i ^ turn) for i in range(4)]
        )
    combined = arrived[:, :2].reshape(2, 4, 2, 4, 2, 256)
    combined = turned_by_core(combined, coil, 1, 1).transpose(4, 1, 3, 0, 2, 5)
    recon = base - step_sizes[0] * combined.reshape(2, 16, 4, 256)
    riders = riders.reshape(4, 768)
    step_grads = jnp.sum(riders[:, 767])[None]
    grads = riders[:, :648].reshape(2592)
    grads = grads.reshape(3, 3, 2, 3, 48).transpose(4, 2, 1, 3, 0)
    return recon, grads[None], step_grads


def solution(mesh):
    return jax.shard_map(
        on_device,
        mesh=mesh,
        in_specs=(
            P(None, "coil", "slab", None),
            P(None, "coil", None, "slab", None),
            P(None, "coil", "slab", None, None),
            P(),
            P(),
            P(),
            P(None, "coil", "slab", None),
        ),
        out_specs=(P(None, "coil", "slab", None), P(), P()),
        check_vma=False,
    )
```

```python
import jax
import jax.numpy as jnp
import numpy as np
from jax import lax
from jax.experimental import pallas as pl
from jax.experimental.pallas import tpu as pltpu
from jax.sharding import PartitionSpec as P

AXES = ("slab", "coil")
BF = jnp.bfloat16
F32 = jnp.float32


def holder(coil, quarter, low):
    z = (low // 4 - 1 + 2 * (coil % 2)) % 4 * 2 + quarter % 2
    return (quarter // 2 * 32 + z * 4 + low % 4) * 4 + coil


def reader(coil, group, low):
    return (group * 16 + low) * 4 + coil


def far_pairs(turn):
    return [
        (holder(c, q, low), reader((q // 2 ^ turn) * 2 + q % 2, c, low))
        for c in range(4)
        for q in range(4)
        for low in range(16)
    ]


def back_pairs(turn):
    return [(to, at) for at, to in far_pairs(turn)]


CORES = [(i, i ^ 1) for i in range(4)]


VM = pl.BlockSpec(memory_space=pltpu.VMEM)
SM = pl.BlockSpec(memory_space=pltpu.SMEM)


def prepare_kernel(where, state, grad, maps, near, next_pair, out):
    for parity in range(2):
        high, low = (near, next_pair) if parity == 0 else (next_pair, near)

        @pl.when(where[1] == parity)
        def _():
            for i in range(2):
                for k in range(2):
                    high[2 * k + i] = state[i, :, 2 + k, :]
                    low[2 * k + i] = state[i, :, k, :]
                high[4 + i] = grad[i, :, 3, :]
                low[4 + i] = grad[i, :, 0, :]

    for part in range(2):
        for c in range(2):
            for r in range(64):
                for h in range(2):
                    first = r * 40 + (part * 2 + c) * 2 + h
                    out[pl.ds(first, 4, stride=8), :] = maps[
                        part, c, r, :, h * 128 : h * 128 + 128
                    ]
    for core in range(2):
        @pl.when(where[0] == core)
        def _():
            for kind in range(2):
                field = (state, grad)[kind]
                for part in range(2):
                    for low in range(16):
                        z = (low // 4 - 1 + 2 * core) % 4
                        for h in range(2):
                            first = (z * 8 + low % 4) * 40 + (16 + kind * 2 + part) * 2 + h
                            rows = field[part, low, :, h * 128 : h * 128 + 128]
                            out[pl.ds(first, 2, stride=160), :] = rows[:2]
                            out[pl.ds(first + 1280, 2, stride=160), :] = rows[2:]


def prepare_call(where, state, grad, maps):
    shape = jax.ShapeDtypeStruct((6, 16, 256), F32)
    return pl.pallas_call(
        prepare_kernel,
        out_shape=(shape, shape, jax.ShapeDtypeStruct((2560, 128), F32)),
        in_specs=[SM, VM, VM, VM],
        out_specs=(VM, VM, VM),
        cost_estimate=pl.CostEstimate(
            flops=0, bytes_accessed=3000000, transcendentals=0
        ),
    )(where, state, grad, maps)


def combine_kernel(quarter, one, two, grad, out):
    product = 0.0
    for k in range(4):
        rows = pl.ds(k, 64, stride=4)
        total = one[rows, :] + two[rows, :]
        out[pl.ds(k, 64, stride=10), :] = total
        product = product + total * grad[rows, :]
    product = jnp.sum(product)
    first = 256 + 6 * quarter[0]
    lane = lax.broadcasted_iota(jnp.int32, (1, 128), 1)
    for k in range(6):
        rider = one[pl.ds(first + k, 1), :] + two[pl.ds(first + k, 1), :]
        if k == 5:
            rider = jnp.where(lane == 127, -product, rider)
        out[pl.ds(4 + k, 64, stride=10), :] = jnp.broadcast_to(rider, (64, 128))


def combine_call(quarter, one, two, grad):
    return pl.pallas_call(
        combine_kernel,
        out_shape=jax.ShapeDtypeStruct((640, 128), F32),
        in_specs=[SM, VM, VM, VM],
        out_specs=VM,
        compiler_params=pltpu.CompilerParams(vmem_limit_bytes=8 << 20),
        cost_estimate=pl.CostEstimate(
            flops=100000, bytes_accessed=800000, transcendentals=0
        ),
    )(quarter, one, two, grad)


def turned_by_core(data, coil, axis, sign):
    even = jnp.roll(data, sign, axis)
    odd = jnp.roll(data, -sign, axis)
    return jnp.where(coil % 2 == 0, even, odd)


def split(value):
    high = value.astype(BF)
    return high, (value - high.astype(F32)).astype(BF)


def split_outside(value):
    high = lax.reduce_precision(value, 8, 7)
    return high.astype(BF), (value - high).astype(BF)


def shifted(value, step):
    if step == 0:
        return value
    lane = lax.broadcasted_iota(jnp.int32, value.shape, value.ndim - 1)
    turned = pltpu.roll(value, step % 256, value.ndim - 1)
    edge = 0 if step > 0 else 255
    return jnp.where(lane == edge, 0.0, turned)


def filter_tables(weights):
    taps = np.zeros((3, 6, 8), np.float32)
    for d in range(3):
        for y in range(6):
            taps[d, y, y + d] = 1.0
    kernel = weights[0]
    ahead = sum(
        kernel[:, :, :, d][:, :, :, :, None, None] * taps[d] for d in range(3)
    )
    ahead = ahead.transpose(4, 0, 3, 2, 1, 5).reshape(288, 144)
    back = np.zeros((3, 4, 6), np.float32)
    for d in range(3):
        for y in range(4):
            back[d, y, y + 2 - d] = 1.0
    behind = sum(
        kernel[:, :, :, d][:, :, :, :, None, None] * back[d] for d in range(3)
    )
    behind = behind.transpose(2, 3, 1, 4, 5, 0).reshape(72, 288)
    high, low = split_outside(ahead)
    wide = jnp.concatenate([high, low, high], axis=1)
    high, low = split_outside(behind)
    turned = jnp.concatenate(
        [
            jnp.concatenate([high, high], axis=1),
            jnp.concatenate([low, jnp.zeros_like(low)], axis=1),
        ],
        axis=0,
    )
    return wide, turned


def window(packed, place, part):
    start = pl.multiple_of(place * 16, 16)
    return jnp.concatenate(
        [packed[d, part, pl.ds(start, 48)] for d in range(3)], axis=0
    )


def forward(place, table, packed):
    high = window(packed, place, 0)
    low = window(packed, place, 1)
    data = jnp.concatenate([high, high, low], axis=0)
    return jnp.dot(table, data, preferred_element_type=F32), high, low


def conv_kernel(
    init, grad, before, after, lower, upper, wide, xb, sums, xs, gs, gb
):
    gs[:, :, 0:1] = jnp.zeros((18, 2, 1, 256), F32)
    gs[:, :, 7:8] = jnp.zeros((18, 2, 1, 256), F32)
    for i in range(2):
        xs[2:18, i, 2:6] = init[i]
        for k in range(2):
            xs[2:18, i, k : k + 1] = before[2 * k + i].reshape(16, 1, 256)
            xs[2:18, i, k + 6 : k + 7] = after[2 * k + i].reshape(16, 1, 256)
        xs[0:2, i] = lower[2 * i : 2 * i + 2]
        xs[18:20, i] = upper[2 * i : 2 * i + 2]
        gs[1:17, i, 2:6] = grad[i]
        gs[1:17, i, 1:2] = before[4 + i].reshape(16, 1, 256)
        gs[1:17, i, 6:7] = after[4 + i].reshape(16, 1, 256)
        gs[0:1, i, 1:7] = lower[4 + i : 5 + i, 0:6]
        gs[17:18, i, 1:7] = upper[4 + i : 5 + i, 0:6]
    for plain, packed, count in ((xs, xb, 320), (gs, gb, 288)):
        value = plain[...].reshape(count, 256)
        for d in range(3):
            high, low = split(shifted(value, 1 - d))
            packed[d, 0] = high
            packed[d, 1] = low
    sums[...] = jnp.zeros_like(sums)

    def step(r, carry):
        response, xh, xl = forward(r + 1, wide[48:240], xb)
        linear, gh, gl = forward(r, wide[48:240], gb)
        core = jnp.tanh(response)
        weighted = (1.0 - core * core) * linear
        ch, cl = split(core)
        wh, wl = split(weighted)
        left = jnp.concatenate([gh, gh, gl, xh, xh, xl], axis=1)
        right = jnp.concatenate([ch, cl, ch, wh, wl, wh], axis=1)
        sums[...] += lax.dot_general(
            left, right, (((1,), (1,)), ((), ())), preferred_element_type=F32
        )
        return carry

    lax.fori_loop(0, 16, step, 0)


def adjoint_kernel(edge, init, xb, wide, turned, base, acc):
    acc[...] = jnp.zeros_like(acc)
    row = lax.broadcasted_iota(jnp.int32, (288, 256), 0)
    keep = jnp.where(row < 48, edge[0], jnp.where(row >= 240, edge[1], 1.0))

    def step(place, carry):
        scale = jnp.where(place == 0, edge[2], jnp.where(place == 17, edge[3], 1.0))
        response, _, _ = forward(place, wide[...], xb)
        high, low = split(jnp.tanh(response) * (keep * scale))
        data = jnp.concatenate([high, low], axis=0)
        product = jnp.dot(turned[...], data, preferred_element_type=F32)
        product = product[:72] + product[72:]
        for r in range(3):
            for d in range(3):
                first = (r * 3 + d) * 8
                acc[d, pl.ds(place + r, 1)] += product[first : first + 8][None]
        return carry

    lax.fori_loop(0, 18, step, 0)
    total = (
        shifted(acc[0, 2:18].reshape(128, 256), -1)
        + acc[1, 2:18].reshape(128, 256)
        + shifted(acc[2, 2:18].reshape(128, 256), 1)
    ).reshape(16, 8, 256)
    for i in range(2):
        base[i] = init[i] - total[:, 4 * i : 4 * i + 4]


def conv_call(init, grad, before, after, lower, upper, wide):
    return pl.pallas_call(
        conv_kernel,
        out_shape=(
            jax.ShapeDtypeStruct((3, 2, 320, 256), BF),
            jax.ShapeDtypeStruct((144, 192), F32),
        ),
        in_specs=[VM] * 7,
        out_specs=(VM, VM),
        scratch_shapes=[
            pltpu.VMEM((20, 2, 8, 256), F32),
            pltpu.VMEM((18, 2, 8, 256), F32),
            pltpu.VMEM((3, 2, 288, 256), BF),
        ],
        cost_estimate=pl.CostEstimate(
            flops=4000000000, bytes_accessed=2000000, transcendentals=800000
        ),
    )(init, grad, before, after, lower, upper, wide)


def adjoint_call(edge, init, xb, wide, turned):
    return pl.pallas_call(
        adjoint_kernel,
        out_shape=jax.ShapeDtypeStruct((2, 16, 4, 256), F32),
        in_specs=[SM] + [VM] * 4,
        out_specs=VM,
        scratch_shapes=[pltpu.VMEM((3, 20, 8, 256), F32)],
        compiler_params=pltpu.CompilerParams(vmem_limit_bytes=20 << 20),
        cost_estimate=pl.CostEstimate(
            flops=4000000000, bytes_accessed=2000000, transcendentals=1300000
        ),
    )(edge, init, xb, wide, turned)


def diagonal(sums):
    cube = sums.reshape(3, 3, 2, 8, 4, 48)
    taps = [
        sum(cube[:, :, :, y + 1 + d, y] for y in range(4)) for d in range(3)
    ]
    return jnp.stack(taps, axis=3)


def tables():
    place = np.arange(256)
    mixed = place % 64 * 4 + place // 64
    made = []
    for first, second in ((place, place), (place, mixed), (mixed, place)):
        angle = (first[:, None] * second[None, :] % 256) * (2.0 * np.pi / 256)
        for table in (np.cos(angle) / 16.0, np.sin(angle) / 16.0):
            table = np.asarray(table, np.float32)
            high = table.astype(BF)
            made.append(high)
            made.append((table - high.astype(np.float32)).astype(BF))
    return np.stack(made)


def transform_kernel(
    coil, maps, p0, p1, p2, p3, kspace, mask, extra, table, kept, sent, rows, right, left, lhs, rhs,
):
    here = coil[0]
    pieces = (p0, p1, p2, p3)

    def slot(a, q):
        return (q // 2 ^ a // 2) + 2 * (q % 2 ^ a % 2)

    for a in range(4):
        @pl.when(here == a)
        def _():
            for q in range(4):
                rows[q] = pieces[slot(a, q)][...]
    for part in range(2):
        cosine, sine = table[part], table[2 + part]
        right[part, :256, :256] = cosine
        right[part, :256, 256:] = -sine
        right[part, 256:, :256] = sine
        right[part, 256:, 256:] = cosine
    for part in range(4):
        first = 4 + part // 2 * 4 + part % 2
        cosine, sine = table[first], table[first + 2]
        left[part, :256, :256] = cosine
        left[part, :256, 256:] = sine
        left[part, 256:, :256] = -sine
        left[part, 256:, 256:] = cosine

    def halves(load):
        return jnp.concatenate(
            [
                jnp.concatenate([load(y, h) for h in range(2)], axis=1)
                for y in range(4)
            ],
            axis=0,
        )

    def map_of(part, c):
        return halves(
            lambda y, h: maps[pl.ds((y * 4 + part * 2 + c) * 2 + h, 64, stride=40), :]
        )

    def image_of(part):
        return halves(lambda y, h: rows[y, pl.ds(part * 2 + h, 64, stride=4), :])

    def transform(pairs, side):
        for c in range(2):
            for part in range(2):
                high, low = split(pairs[c][part])
                lhs[0, c * 256 : c * 256 + 256, part * 256 : part * 256 + 256] = high
                lhs[1, c * 256 : c * 256 + 256, part * 256 : part * 256 + 256] = low
        for c in range(2):
            block = slice(c * 256, c * 256 + 256)
            value = (
                jnp.dot(lhs[0, block], right[0], preferred_element_type=F32)
                + jnp.dot(lhs[1, block], right[0], preferred_element_type=F32)
                + jnp.dot(lhs[0, block], right[1], preferred_element_type=F32)
            )
            for part in range(2):
                high, low = split(value[:, part * 256 : part * 256 + 256])
                rhs[0, part * 256 : part * 256 + 256, block] = high
                rhs[1, part * 256 : part * 256 + 256, block] = low
        out = []
        for part in range(2):
            block = slice(part * 256, part * 256 + 256)
            out.append(
                jnp.dot(left[side, block], rhs[0], preferred_element_type=F32)
                + jnp.dot(left[side, block], rhs[1], preferred_element_type=F32)
                + jnp.dot(left[side + 1, block], rhs[0], preferred_element_type=F32)
            )
        return [
            [out[part][:, c * 256 : c * 256 + 256] for part in range(2)]
            for c in range(2)
        ]

    vr, vi = image_of(0), image_of(1)
    pairs = []
    for c in range(2):
        sr, si = map_of(0, c), map_of(1, c)
        pairs.append([sr * vr - si * vi, sr * vi + si * vr])
    pairs = transform(pairs, 0)
    keep = mask[...].astype(F32)

    pairs = [
        [
            (pairs[c][0] - kspace[0, c]) * keep,
            (kspace[1, c] - pairs[c][1]) * keep,
        ]
        for c in range(2)
    ]
    pairs = transform(pairs, 2)
    back_re = 0.0
    back_im = 0.0
    for c in range(2):
        sr, si = map_of(0, c), map_of(1, c)
        xr, xi = pairs[c][0], -pairs[c][1]
        back_re = back_re + sr * xr + si * xi
        back_im = back_im + sr * xi - si * xr
    back = (back_re, back_im)
    for out in (kept, sent):
        for t in range(2):
            out[t, 256:280] = extra[...]
    for a in range(4):
        @pl.when(here == a)
        def _():
            for q in range(4):
                place = slot(a, q)
                out = sent if place >= 2 else kept
                for part in range(2):
                    for h in range(2):
                        out[place % 2, pl.ds(part * 2 + h, 64, stride=4), :] = back[
                            part
                        ][q * 64 : q * 64 + 64, h * 128 : h * 128 + 128]


def transform_call(coil, maps, pieces, kspace, mask, extra, table):
    vm = pl.BlockSpec(memory_space=pltpu.VMEM)
    return pl.pallas_call(
        transform_kernel,
        out_shape=tuple(jax.ShapeDtypeStruct((2, 280, 128), F32) for _ in range(2)),
        in_specs=[pl.BlockSpec(memory_space=pltpu.SMEM)] + [vm] * 9,
        out_specs=(vm,) * 2,
        scratch_shapes=[
            pltpu.VMEM((4, 256, 128), F32),
            pltpu.VMEM((2, 512, 512), BF),
            pltpu.VMEM((4, 512, 512), BF),
            pltpu.VMEM((2, 512, 512), BF),
            pltpu.VMEM((2, 512, 512), BF),
        ],
        compiler_params=pltpu.CompilerParams(vmem_limit_bytes=32 << 20),
        cost_estimate=pl.CostEstimate(
            flops=6000000000, bytes_accessed=5000000, transcendentals=0
        ),
    )(coil, maps, *pieces, kspace, mask, extra, table)


def swapped(first, second):
    return [(first, second), (second, first)]


def halos(state, grad, near, far, slab_count):
    odd = lax.axis_index("slab") % 2
    pairs = [p for i in range(0, slab_count, 2) for p in swapped(i, i + 1)]
    others = [p for i in range(1, slab_count - 1, 2) for p in swapped(i, i + 1)]
    near = lax.ppermute(near, "slab", pairs)
    far = lax.ppermute(far, "slab", others)
    before = jnp.where(odd == 0, far, near)
    after = jnp.where(odd == 0, near, far)

    def planes(at, last):
        head = before[:4, at].reshape(2, 2, 2, 256).transpose(1, 2, 0, 3)
        tail = after[:4, at].reshape(2, 2, 2, 256).transpose(1, 2, 0, 3)
        rows = jnp.concatenate([head, state[:, at], tail], axis=2).reshape(4, 8, 256)
        edge = jnp.concatenate(
            [before[4:, last, None], grad[:, last], after[4:, last, None]], axis=1
        )
        return jnp.concatenate([rows, jnp.pad(edge, ((0, 0), (0, 2), (0, 0)))], axis=0)

    odd = lax.axis_index("coil") % 2
    high, low = planes(slice(14, 16), 15), planes(slice(0, 2), 0)
    near = lax.ppermute(jnp.where(odd == 0, high, low), "coil", CORES)
    far = lax.ppermute(jnp.where(odd == 0, low, high), "coil", swapped(1, 2))
    lower = jnp.where(odd == 0, far, near)
    upper = jnp.where(odd == 0, near, far)
    return before, after, lower, upper


def on_device(init_image, sens, kspace, mask, weights, step_sizes, recon_cotangent):
    slab_count = lax.axis_size("slab")
    coil = lax.axis_index("coil")
    slab = lax.axis_index("slab")
    near, far, payload = prepare_call(
        jnp.stack([coil % 2, slab % 2]), init_image, recon_cotangent, sens
    )
    payload = payload.reshape(64, 20, 2, 128)
    received = lax.all_to_all(payload, "slab", split_axis=0, concat_axis=0, tiled=True)

    before, after, lower, upper = halos(
        init_image, recon_cotangent, near, far, slab_count
    )
    wide, turned = filter_tables(weights)
    edge = jnp.stack([slab > 0, slab < slab_count - 1, coil > 0, coil < 3]).astype(F32)
    table = jnp.asarray(tables())
    lower, wide, turned, edge, table = lax.optimization_barrier(
        (lower, wide, turned, edge, table)
    )
    packed, sums = conv_call(
        init_image, recon_cotangent, before, after, lower, upper, wide
    )
    extra = jnp.pad(-diagonal(sums).reshape(4, 648), ((0, 0), (0, 120)))
    extra = extra.reshape(24, 128)

    held = received[:, 16:18].reshape(256, 128)
    pieces = []
    for turn in range(2):
        pieces.append(lax.ppermute(held, AXES, far_pairs(turn)))
    pieces = pieces + [lax.ppermute(piece, "coil", CORES) for piece in pieces]
    kept, sent = transform_call(
        coil.reshape(1), received.reshape(2560, 128), pieces, kspace[:, :, 0], mask,
        extra, table,
    )
    kept = kept + lax.ppermute(sent, "coil", CORES)
    parts = []
    for turn in range(2):
        parts.append(lax.ppermute(kept[turn], AXES, back_pairs(turn)))
    quarter = slab // 32 * 2 + slab // 4 % 2
    sent = combine_call(
        quarter.reshape(1), *parts, received[:, 18:20].reshape(256, 128)
    )
    sent = sent.reshape(64, 5, 2, 128)
    arrived = lax.all_to_all(sent, "slab", split_axis=0, concat_axis=0, tiled=True)
    base = adjoint_call(edge, init_image, packed, wide, turned)
    own = jnp.sum(arrived[:, 2:].reshape(2, 4, 2, 4, 6, 128), axis=(1, 3))
    own = own.reshape(24, 128)
    riders = own
    for turn in range(1, 4):
        riders = riders + lax.ppermute(
            own, "coil", [(i, i ^ turn) for i in range(4)]
        )
    combined = arrived[:, :2].reshape(2, 4, 2, 4, 2, 256)
    combined = turned_by_core(combined, coil, 1, 1).transpose(4, 1, 3, 0, 2, 5)
    recon = base - step_sizes[0] * combined.reshape(2, 16, 4, 256)
    riders = riders.reshape(4, 768)
    step_grads = jnp.sum(riders[:, 767])[None]
    grads = riders[:, :648].reshape(2592)
    grads = grads.reshape(3, 3, 2, 3, 48).transpose(4, 2, 1, 3, 0)
    return recon, grads[None], step_grads


def solution(mesh):
    return jax.shard_map(
        on_device,
        mesh=mesh,
        in_specs=(
            P(None, "coil", "slab", None),
            P(None, "coil", None, "slab", None),
            P(None, "coil", "slab", None, None),
            P(),
            P(),
            P(),
            P(None, "coil", "slab", None),
        ),
        out_specs=(P(None, "coil", "slab", None), P(), P()),
        check_vma=False,
    )
```

```python
import jax
import jax.numpy as jnp
import numpy as np
from jax import lax
from jax.experimental import pallas as pl
from jax.experimental.pallas import tpu as pltpu
from jax.sharding import PartitionSpec as P

AXES = ("slab", "coil")
BF = jnp.bfloat16
F32 = jnp.float32


def holder(coil, quarter, low):
    z = (low // 4 - 1 + 2 * (coil % 2)) % 4 * 2 + quarter % 2
    return (quarter // 2 * 32 + z * 4 + low % 4) * 4 + coil


def reader(coil, group, low):
    return (group * 16 + low) * 4 + coil


def far_pairs(turn):
    return [
        (holder(c, q, low), reader((q // 2 ^ turn) * 2 + q % 2, c, low))
        for c in range(4)
        for q in range(4)
        for low in range(16)
    ]


def back_pairs(turn):
    return [(to, at) for at, to in far_pairs(turn)]


CORES = [(i, i ^ 1) for i in range(4)]


VM = pl.BlockSpec(memory_space=pltpu.VMEM)
SM = pl.BlockSpec(memory_space=pltpu.SMEM)


def prepare_kernel(coil, slab, state, grad, maps, near, next_pair, out):
    for parity in range(2):
        high, low = (near, next_pair) if parity == 0 else (next_pair, near)

        @pl.when(slab[0] % 2 == parity)
        def _():
            for i in range(2):
                for k in range(2):
                    high[2 * k + i] = state[i, :, 2 + k, :]
                    low[2 * k + i] = state[i, :, k, :]
                high[4 + i] = grad[i, :, 3, :]
                low[4 + i] = grad[i, :, 0, :]

    for part in range(2):
        for c in range(2):
            for r in range(64):
                for h in range(2):
                    first = r * 40 + (part * 2 + c) * 2 + h
                    out[pl.ds(first, 4, stride=8), :] = maps[
                        part, c, r, :, h * 128 : h * 128 + 128
                    ]
    for core in range(2):
        @pl.when(coil[0] % 2 == core)
        def _():
            for kind in range(2):
                field = (state, grad)[kind]
                for part in range(2):
                    for low in range(16):
                        z = (low // 4 - 1 + 2 * core) % 4
                        for h in range(2):
                            first = (z * 8 + low % 4) * 40 + (16 + kind * 2 + part) * 2 + h
                            rows = field[part, low, :, h * 128 : h * 128 + 128]
                            out[pl.ds(first, 2, stride=160), :] = rows[:2]
                            out[pl.ds(first + 1280, 2, stride=160), :] = rows[2:]


def prepare_call(coil, slab, state, grad, maps):
    shape = jax.ShapeDtypeStruct((6, 16, 256), F32)
    return pl.pallas_call(
        prepare_kernel,
        out_shape=(shape, shape, jax.ShapeDtypeStruct((2560, 128), F32)),
        in_specs=[SM, SM, VM, VM, VM],
        out_specs=(VM, VM, VM),
        cost_estimate=pl.CostEstimate(
            flops=0, bytes_accessed=3000000, transcendentals=0
        ),
    )(coil, slab, state, grad, maps)


def combine_kernel(quarter, one, two, grad, out):
    product = 0.0
    for k in range(4):
        rows = pl.ds(k, 64, stride=4)
        total = one[rows, :] + two[rows, :]
        out[pl.ds(k, 64, stride=10), :] = total
        product = product + total * grad[rows, :]
    product = jnp.sum(product)
    first = 256 + 6 * quarter[0]
    lane = lax.broadcasted_iota(jnp.int32, (1, 128), 1)
    for k in range(6):
        rider = one[pl.ds(first + k, 1), :] + two[pl.ds(first + k, 1), :]
        if k == 5:
            rider = jnp.where(lane == 127, -product, rider)
        out[pl.ds(4 + k, 64, stride=10), :] = jnp.broadcast_to(rider, (64, 128))


def combine_call(quarter, one, two, grad):
    return pl.pallas_call(
        combine_kernel,
        out_shape=jax.ShapeDtypeStruct((640, 128), F32),
        in_specs=[SM, VM, VM, VM],
        out_specs=VM,
        compiler_params=pltpu.CompilerParams(vmem_limit_bytes=8 << 20),
        cost_estimate=pl.CostEstimate(
            flops=100000, bytes_accessed=800000, transcendentals=0
        ),
    )(quarter, one, two, grad)


def turned_by_core(data, coil, axis, sign):
    even = jnp.roll(data, sign, axis)
    odd = jnp.roll(data, -sign, axis)
    return jnp.where(coil % 2 == 0, even, odd)


def split(value):
    high = value.astype(BF)
    return high, (value - high.astype(F32)).astype(BF)


def split_outside(value):
    high = lax.reduce_precision(value, 8, 7)
    return high.astype(BF), (value - high).astype(BF)


def shifted(value, step):
    if step == 0:
        return value
    lane = lax.broadcasted_iota(jnp.int32, value.shape, value.ndim - 1)
    turned = pltpu.roll(value, step % 256, value.ndim - 1)
    edge = 0 if step > 0 else 255
    return jnp.where(lane == edge, 0.0, turned)


def filter_tables(weights):
    taps = np.zeros((3, 6, 8), np.float32)
    for d in range(3):
        for y in range(6):
            taps[d, y, y + d] = 1.0
    kernel = weights[0]
    ahead = sum(
        kernel[:, :, :, d][:, :, :, :, None, None] * taps[d] for d in range(3)
    )
    ahead = ahead.transpose(4, 0, 3, 2, 1, 5).reshape(288, 144)
    back = np.zeros((3, 4, 6), np.float32)
    for d in range(3):
        for y in range(4):
            back[d, y, y + 2 - d] = 1.0
    behind = sum(
        kernel[:, :, :, d][:, :, :, :, None, None] * back[d] for d in range(3)
    )
    behind = behind.transpose(2, 3, 1, 4, 5, 0).reshape(72, 288)
    high, low = split_outside(ahead)
    wide = jnp.concatenate([high, low, high], axis=1)
    high, low = split_outside(behind)
    turned = jnp.concatenate(
        [
            jnp.concatenate([high, high], axis=1),
            jnp.concatenate([low, jnp.zeros_like(low)], axis=1),
        ],
        axis=0,
    )
    return wide, turned


def window(packed, place, part):
    start = pl.multiple_of(place * 16, 16)
    return jnp.concatenate(
        [packed[d, part, pl.ds(start, 48)] for d in range(3)], axis=0
    )


def forward(place, table, packed):
    high = window(packed, place, 0)
    low = window(packed, place, 1)
    data = jnp.concatenate([high, high, low], axis=0)
    return jnp.dot(table, data, preferred_element_type=F32), high, low


def conv_kernel(
    init, grad, before, after, lower, upper, wide, xb, sums, xs, gs, gb
):
    gs[:, :, 0:1] = jnp.zeros((18, 2, 1, 256), F32)
    gs[:, :, 7:8] = jnp.zeros((18, 2, 1, 256), F32)
    for i in range(2):
        xs[2:18, i, 2:6] = init[i]
        for k in range(2):
            xs[2:18, i, k : k + 1] = before[2 * k + i].reshape(16, 1, 256)
            xs[2:18, i, k + 6 : k + 7] = after[2 * k + i].reshape(16, 1, 256)
        xs[0:2, i] = lower[2 * i : 2 * i + 2]
        xs[18:20, i] = upper[2 * i : 2 * i + 2]
        gs[1:17, i, 2:6] = grad[i]
        gs[1:17, i, 1:2] = before[4 + i].reshape(16, 1, 256)
        gs[1:17, i, 6:7] = after[4 + i].reshape(16, 1, 256)
        gs[0:1, i, 1:7] = lower[4 + i : 5 + i, 0:6]
        gs[17:18, i, 1:7] = upper[4 + i : 5 + i, 0:6]
    for plain, packed, count in ((xs, xb, 320), (gs, gb, 288)):
        value = plain[...].reshape(count, 256)
        for d in range(3):
            high, low = split(shifted(value, 1 - d))
            packed[d, 0] = high
            packed[d, 1] = low
    sums[...] = jnp.zeros_like(sums)

    def step(r, carry):
        response, xh, xl = forward(r + 1, wide[48:240], xb)
        linear, gh, gl = forward(r, wide[48:240], gb)
        core = jnp.tanh(response)
        weighted = (1.0 - core * core) * linear
        ch, cl = split(core)
        wh, wl = split(weighted)
        left = jnp.concatenate([gh, gh, gl, xh, xh, xl], axis=1)
        right = jnp.concatenate([ch, cl, ch, wh, wl, wh], axis=1)
        sums[...] += lax.dot_general(
            left, right, (((1,), (1,)), ((), ())), preferred_element_type=F32
        )
        return carry

    lax.fori_loop(0, 16, step, 0)


def adjoint_kernel(edge, init, xb, wide, turned, base, acc):
    acc[...] = jnp.zeros_like(acc)
    row = lax.broadcasted_iota(jnp.int32, (288, 256), 0)
    keep = jnp.where(row < 48, edge[0], jnp.where(row >= 240, edge[1], 1.0))

    def step(place, carry):
        scale = jnp.where(place == 0, edge[2], jnp.where(place == 17, edge[3], 1.0))
        response, _, _ = forward(place, wide[...], xb)
        high, low = split(jnp.tanh(response) * (keep * scale))
        data = jnp.concatenate([high, low], axis=0)
        product = jnp.dot(turned[...], data, preferred_element_type=F32)
        product = product[:72] + product[72:]
        for r in range(3):
            for d in range(3):
                first = (r * 3 + d) * 8
                acc[d, pl.ds(place + r, 1)] += product[first : first + 8][None]
        return carry

    lax.fori_loop(0, 18, step, 0)
    total = (
        shifted(acc[0, 2:18].reshape(128, 256), -1)
        + acc[1, 2:18].reshape(128, 256)
        + shifted(acc[2, 2:18].reshape(128, 256), 1)
    ).reshape(16, 8, 256)
    for i in range(2):
        base[i] = init[i] - total[:, 4 * i : 4 * i + 4]


def conv_call(init, grad, before, after, lower, upper, wide):
    return pl.pallas_call(
        conv_kernel,
        out_shape=(
            jax.ShapeDtypeStruct((3, 2, 320, 256), BF),
            jax.ShapeDtypeStruct((144, 192), F32),
        ),
        in_specs=[VM] * 7,
        out_specs=(VM, VM),
        scratch_shapes=[
            pltpu.VMEM((20, 2, 8, 256), F32),
            pltpu.VMEM((18, 2, 8, 256), F32),
            pltpu.VMEM((3, 2, 288, 256), BF),
        ],
        cost_estimate=pl.CostEstimate(
            flops=4000000000, bytes_accessed=2000000, transcendentals=800000
        ),
    )(init, grad, before, after, lower, upper, wide)


def adjoint_call(edge, init, xb, wide, turned):
    return pl.pallas_call(
        adjoint_kernel,
        out_shape=jax.ShapeDtypeStruct((2, 16, 4, 256), F32),
        in_specs=[SM] + [VM] * 4,
        out_specs=VM,
        scratch_shapes=[pltpu.VMEM((3, 20, 8, 256), F32)],
        compiler_params=pltpu.CompilerParams(vmem_limit_bytes=20 << 20),
        cost_estimate=pl.CostEstimate(
            flops=4000000000, bytes_accessed=2000000, transcendentals=1300000
        ),
    )(edge, init, xb, wide, turned)


def diagonal(sums):
    cube = sums.reshape(3, 3, 2, 8, 4, 48)
    taps = [
        sum(cube[:, :, :, y + 1 + d, y] for y in range(4)) for d in range(3)
    ]
    return jnp.stack(taps, axis=3)


def tables():
    place = np.arange(256)
    mixed = place % 64 * 4 + place // 64
    made = []
    for first, second in ((place, place), (place, mixed), (mixed, place)):
        angle = (first[:, None] * second[None, :] % 256) * (2.0 * np.pi / 256)
        for table in (np.cos(angle) / 16.0, np.sin(angle) / 16.0):
            table = np.asarray(table, np.float32)
            high = table.astype(BF)
            made.append(high)
            made.append((table - high.astype(np.float32)).astype(BF))
    return np.stack(made)


def transform_kernel(
    coil, maps, p0, p1, p2, p3, kspace, mask, extra, table, kept, sent, rows, right, left, lhs, rhs,
):
    here = coil[0]
    pieces = (p0, p1, p2, p3)

    def slot(a, q):
        return (q // 2 ^ a // 2) + 2 * (q % 2 ^ a % 2)

    for a in range(4):
        @pl.when(here == a)
        def _():
            for q in range(4):
                rows[q] = pieces[slot(a, q)][...]
    for part in range(2):
        cosine, sine = table[part], table[2 + part]
        right[part, :256, :256] = cosine
        right[part, :256, 256:] = -sine
        right[part, 256:, :256] = sine
        right[part, 256:, 256:] = cosine
    for part in range(4):
        first = 4 + part // 2 * 4 + part % 2
        cosine, sine = table[first], table[first + 2]
        left[part, :256, :256] = cosine
        left[part, :256, 256:] = sine
        left[part, 256:, :256] = -sine
        left[part, 256:, 256:] = cosine

    def halves(load):
        return jnp.concatenate(
            [
                jnp.concatenate([load(y, h) for h in range(2)], axis=1)
                for y in range(4)
            ],
            axis=0,
        )

    def map_of(part, c):
        return halves(
            lambda y, h: maps[pl.ds((y * 4 + part * 2 + c) * 2 + h, 64, stride=40), :]
        )

    def image_of(part):
        return halves(lambda y, h: rows[y, pl.ds(part * 2 + h, 64, stride=4), :])

    def transform(pairs, side):
        for c in range(2):
            for part in range(2):
                high, low = split(pairs[c][part])
                lhs[0, c * 256 : c * 256 + 256, part * 256 : part * 256 + 256] = high
                lhs[1, c * 256 : c * 256 + 256, part * 256 : part * 256 + 256] = low
        for c in range(2):
            block = slice(c * 256, c * 256 + 256)
            value = (
                jnp.dot(lhs[0, block], right[0], preferred_element_type=F32)
                + jnp.dot(lhs[1, block], right[0], preferred_element_type=F32)
                + jnp.dot(lhs[0, block], right[1], preferred_element_type=F32)
            )
            for part in range(2):
                high, low = split(value[:, part * 256 : part * 256 + 256])
                rhs[0, part * 256 : part * 256 + 256, block] = high
                rhs[1, part * 256 : part * 256 + 256, block] = low
        out = []
        for part in range(2):
            block = slice(part * 256, part * 256 + 256)
            out.append(
                jnp.dot(left[side, block], rhs[0], preferred_element_type=F32)
                + jnp.dot(left[side, block], rhs[1], preferred_element_type=F32)
                + jnp.dot(left[side + 1, block], rhs[0], preferred_element_type=F32)
            )
        return [
            [out[part][:, c * 256 : c * 256 + 256] for part in range(2)]
            for c in range(2)
        ]

    vr, vi = image_of(0), image_of(1)
    pairs = []
    for c in range(2):
        sr, si = map_of(0, c), map_of(1, c)
        pairs.append([sr * vr - si * vi, sr * vi + si * vr])
    pairs = transform(pairs, 0)
    keep = mask[...].astype(F32)

    pairs = [
        [
            (pairs[c][0] - kspace[0, c]) * keep,
            (kspace[1, c] - pairs[c][1]) * keep,
        ]
        for c in range(2)
    ]
    pairs = transform(pairs, 2)
    back_re = 0.0
    back_im = 0.0
    for c in range(2):
        sr, si = map_of(0, c), map_of(1, c)
        xr, xi = pairs[c][0], -pairs[c][1]
        back_re = back_re + sr * xr + si * xi
        back_im = back_im + sr * xi - si * xr
    back = (back_re, back_im)
    for out in (kept, sent):
        for t in range(2):
            out[t, 256:280] = extra[...]
    for a in range(4):
        @pl.when(here == a)
        def _():
            for q in range(4):
                place = slot(a, q)
                out = sent if place >= 2 else kept
                for part in range(2):
                    for h in range(2):
                        out[place % 2, pl.ds(part * 2 + h, 64, stride=4), :] = back[
                            part
                        ][q * 64 : q * 64 + 64, h * 128 : h * 128 + 128]


def transform_call(coil, maps, pieces, kspace, mask, extra, table):
    vm = pl.BlockSpec(memory_space=pltpu.VMEM)
    return pl.pallas_call(
        transform_kernel,
        out_shape=tuple(jax.ShapeDtypeStruct((2, 280, 128), F32) for _ in range(2)),
        in_specs=[pl.BlockSpec(memory_space=pltpu.SMEM)] + [vm] * 9,
        out_specs=(vm,) * 2,
        scratch_shapes=[
            pltpu.VMEM((4, 256, 128), F32),
            pltpu.VMEM((2, 512, 512), BF),
            pltpu.VMEM((4, 512, 512), BF),
            pltpu.VMEM((2, 512, 512), BF),
            pltpu.VMEM((2, 512, 512), BF),
        ],
        compiler_params=pltpu.CompilerParams(vmem_limit_bytes=32 << 20),
        cost_estimate=pl.CostEstimate(
            flops=6000000000, bytes_accessed=5000000, transcendentals=0
        ),
    )(coil, maps, *pieces, kspace, mask, extra, table)


def swapped(first, second):
    return [(first, second), (second, first)]


def halos(state, grad, near, far, slab_count):
    odd = lax.axis_index("slab") % 2
    pairs = [p for i in range(0, slab_count, 2) for p in swapped(i, i + 1)]
    others = [p for i in range(1, slab_count - 1, 2) for p in swapped(i, i + 1)]
    near = lax.ppermute(near, "slab", pairs)
    far = lax.ppermute(far, "slab", others)
    before = jnp.where(odd == 0, far, near)
    after = jnp.where(odd == 0, near, far)

    def planes(at, last):
        head = before[:4, at].reshape(2, 2, 2, 256).transpose(1, 2, 0, 3)
        tail = after[:4, at].reshape(2, 2, 2, 256).transpose(1, 2, 0, 3)
        rows = jnp.concatenate([head, state[:, at], tail], axis=2).reshape(4, 8, 256)
        edge = jnp.concatenate(
            [before[4:, last, None], grad[:, last], after[4:, last, None]], axis=1
        )
        return jnp.concatenate([rows, jnp.pad(edge, ((0, 0), (0, 2), (0, 0)))], axis=0)

    odd = lax.axis_index("coil") % 2
    high, low = planes(slice(14, 16), 15), planes(slice(0, 2), 0)
    near = lax.ppermute(jnp.where(odd == 0, high, low), "coil", CORES)
    far = lax.ppermute(jnp.where(odd == 0, low, high), "coil", swapped(1, 2))
    lower = jnp.where(odd == 0, far, near)
    upper = jnp.where(odd == 0, near, far)
    return before, after, lower, upper


def on_device(init_image, sens, kspace, mask, weights, step_sizes, recon_cotangent):
    slab_count = lax.axis_size("slab")
    coil = lax.axis_index("coil")
    slab = lax.axis_index("slab")
    near, far, payload = prepare_call(
        coil.reshape(1), slab.reshape(1), init_image, recon_cotangent, sens
    )
    payload = payload.reshape(64, 20, 2, 128)
    received = lax.all_to_all(payload, "slab", split_axis=0, concat_axis=0, tiled=True)

    before, after, lower, upper = halos(
        init_image, recon_cotangent, near, far, slab_count
    )
    wide, turned = filter_tables(weights)
    edge = jnp.stack([slab > 0, slab < slab_count - 1, coil > 0, coil < 3]).astype(F32)
    table = jnp.asarray(tables())
    lower, wide, turned, edge, table = lax.optimization_barrier(
        (lower, wide, turned, edge, table)
    )
    packed, sums = conv_call(
        init_image, recon_cotangent, before, after, lower, upper, wide
    )
    extra = jnp.pad(-diagonal(sums).reshape(4, 648), ((0, 0), (0, 120)))
    extra = extra.reshape(24, 128)

    held = received[:, 16:18].reshape(256, 128)
    pieces = []
    for turn in range(2):
        pieces.append(lax.ppermute(held, AXES, far_pairs(turn)))
    pieces = pieces + [lax.ppermute(piece, "coil", CORES) for piece in pieces]
    kept, sent = transform_call(
        coil.reshape(1), received.reshape(2560, 128), pieces, kspace[:, :, 0], mask,
        extra, table,
    )
    kept = kept + lax.ppermute(sent, "coil", CORES)
    parts = []
    for turn in range(2):
        parts.append(lax.ppermute(kept[turn], AXES, back_pairs(turn)))
    quarter = slab // 32 * 2 + slab // 4 % 2
    sent = combine_call(
        quarter.reshape(1), *parts, received[:, 18:20].reshape(256, 128)
    )
    sent = sent.reshape(64, 5, 2, 128)
    arrived = lax.all_to_all(sent, "slab", split_axis=0, concat_axis=0, tiled=True)
    base = adjoint_call(edge, init_image, packed, wide, turned)
    own = jnp.sum(arrived[:, 2:].reshape(2, 4, 2, 4, 6, 128), axis=(1, 3))
    own = own.reshape(24, 128)
    riders = own
    for turn in range(1, 4):
        riders = riders + lax.ppermute(
            own, "coil", [(i, i ^ turn) for i in range(4)]
        )
    combined = arrived[:, :2].reshape(2, 4, 2, 4, 2, 256)
    combined = turned_by_core(combined, coil, 1, 1).transpose(4, 1, 3, 0, 2, 5)
    recon = base - step_sizes[0] * combined.reshape(2, 16, 4, 256)
    riders = riders.reshape(4, 768)
    step_grads = jnp.sum(riders[:, 767])[None]
    grads = riders[:, :648].reshape(2592)
    grads = grads.reshape(3, 3, 2, 3, 48).transpose(4, 2, 1, 3, 0)
    return recon, grads[None], step_grads


def solution(mesh):
    return jax.shard_map(
        on_device,
        mesh=mesh,
        in_specs=(
            P(None, "coil", "slab", None),
            P(None, "coil", None, "slab", None),
            P(None, "coil", "slab", None, None),
            P(),
            P(),
            P(),
            P(None, "coil", "slab", None),
        ),
        out_specs=(P(None, "coil", "slab", None), P(), P()),
        check_vma=False,
    )
```
